512 devices in a mesh: gy: 16 (over x_hi, y, core), gx: 32 (over z, x_lo).
Axes of the slice: x: 4 (x_hi: 2, x_lo: 2; x = x_hi * 2 + x_lo), y: 4, z: 16, core: 2. Of those that a mesh axis runs over, the one named last changes fastest.
Arguments:
- embeddings: bfloat16 [128, 4096, 128], P('gy', 'gx'), may hold values from -180 to 180
- affinity: float32 [4, 128, 4096], P(None, 'gy', 'gx'), may hold values from 0 to 1, as said below
- assignment: int32 [128, 4096], P('gy', 'gx'), may hold values from 0 to 1023
Outputs:
- min_distance: float32 [128, 4096], P('gy', 'gx')
- new_centroids: float32 [1024, 128], replicated
The draws below stay inside these ranges and needn't reach their ends.
Inputs may be any that keep to these rules, and one draw needn't show every extreme that they name: `affinity`: weight 0 exactly for edges that leave the slab; every other edge weighs 0.05 or more.
All inputs are finite; a program needn't handle non-finite values.
Results may differ from the reference program's by a relative error of at most 0.00045.
Values may be sent and summed in bfloat16 or wider, within the bound.
No kernel may reach another device: no remote copies, remote signals or barrier semaphores. Data moves between devices by JAX's collectives and lax.ppermute only.
A program may use at most 64 MiB of HBM per device.

```python
import math
import jax
import jax.numpy as jnp
from jax import lax

C = 128
K = 1024
DEGREE = 4
TH = 8
TW = 128
NH = 128
NW = 4096
NPIX = 524288
LOCAL = 2


def label_field(key):
    base = jax.random.fold_in(key, 11)
    rows = jnp.arange(NH, dtype=jnp.int32)[:, None]
    cols = jnp.arange(NW, dtype=jnp.int32)[None, :]
    home = rows // TH * (NW // TW) + cols // TW
    nearby = home * LOCAL + jax.random.randint(jax.random.fold_in(base, 1), (NH, NW), 0, LOCAL)
    anywhere = jax.random.randint(jax.random.fold_in(base, 2), (NH, NW), 0, K)
    picker = jax.random.randint(jax.random.fold_in(base, 3), (NH, NW), 0, 5)
    return jnp.where(picker == 0, anywhere, nearby).astype(jnp.int32)


def draw_assignment(key, part):
    return label_field(key)


def draw_embeddings(key, part):
    labels = label_field(key)
    base = jax.random.fold_in(key, 23)
    centres = jax.random.truncated_normal(jax.random.fold_in(base, 1), -3.0, 3.0, (K, C), jnp.float32)
    noise = jax.random.truncated_normal(jax.random.fold_in(base, 2), -4.0, 4.0, (NH, NW, C), jnp.float32)
    pixel_scale = jnp.exp(jax.random.uniform(jax.random.fold_in(base, 3), (NH, NW, 1), jnp.float32, 0.0, math.log(10.0)))
    channel_scale = jnp.exp(jax.random.uniform(jax.random.fold_in(base, 4), (1, 1, C), jnp.float32, 0.0, math.log(10.0)))
    rising = jnp.exp(math.log(3.0) * jnp.arange(NH, dtype=jnp.float32)[:, None, None] / NH)
    values = (centres[labels] + 0.7 * noise) * pixel_scale * channel_scale * rising * 0.1
    return values.astype(jnp.bfloat16)


def draw_affinity(key, part):
    base = jax.random.fold_in(key, 37)
    values = jnp.exp(jax.random.uniform(base, (4, NH, NW), jnp.float32, math.log(0.05), 0.0))
    rows = jnp.arange(NH, dtype=jnp.int32)[:, None]
    cols = jnp.arange(NW, dtype=jnp.int32)[None, :]
    right_in = jnp.broadcast_to(cols < NW - 1, (NH, NW))
    below_in = jnp.broadcast_to(rows < NH - 1, (NH, NW))
    left_in = jnp.broadcast_to(cols > 0, (NH, NW))
    keeper = jnp.stack([right_in, below_in, below_in & right_in, below_in & left_in])
    return jnp.where(keeper, values, 0.0).astype(jnp.float32)


def setup_inputs(seed: int = 0) -> dict:
    streams_of = jax.random.split(jax.random.key(seed), 4)
    return {
        "embeddings": draw_embeddings(jax.random.fold_in(streams_of[3], 71), 0),
        "affinity": draw_affinity(jax.random.fold_in(streams_of[3], 71), 0),
        "assignment": draw_assignment(jax.random.fold_in(streams_of[3], 71), 0),
    }


COEFFS = (0.5, 0.45, 0.35, 0.25, 0.15)

def degree_of(w_ext):
    w_east, w_south, w_diag, w_anti = (w_ext[0], w_ext[1], w_ext[2], w_ext[3])
    result = w_east[1:-1, 1:-1] + w_east[1:-1, :-2]
    result = result + w_south[1:-1, 1:-1] + w_south[:-2, 1:-1]
    result = result + w_diag[1:-1, 1:-1] + w_diag[:-2, :-2]
    return result + w_anti[1:-1, 1:-1] + w_anti[:-2, 2:]

def edge_sum(w_ext, field):
    w_east, w_south, w_diag, w_anti = (w_ext[0], w_ext[1], w_ext[2], w_ext[3])
    result = w_east[1:-1, 1:-1, None] * field[1:-1, 2:]
    result = result + w_east[1:-1, :-2, None] * field[1:-1, :-2]
    result = result + w_south[1:-1, 1:-1, None] * field[2:, 1:-1]
    result = result + w_south[:-2, 1:-1, None] * field[:-2, 1:-1]
    result = result + w_diag[1:-1, 1:-1, None] * field[2:, 2:]
    result = result + w_diag[:-2, :-2, None] * field[:-2, :-2]
    result = result + w_anti[1:-1, 1:-1, None] * field[2:, :-2]
    return result + w_anti[:-2, 2:, None] * field[:-2, 2:]

def whitening(gram, count):
    lower = jnp.linalg.cholesky(gram)
    identity = jnp.eye(gram.shape[0], dtype=gram.dtype)
    inverse = jax.scipy.linalg.solve_triangular(lower, identity, lower=True)
    return math.sqrt(count) * inverse.T

def reference(embeddings, affinity, assignment):
    padded_w = jnp.pad(affinity, ((0, 0), (1, 1), (1, 1)))
    scale = lax.rsqrt(degree_of(padded_w))[..., None]

    def apply_op(field):
        moved = jnp.pad(scale * field, ((1, 1), (1, 1), (0, 0)))
        return scale * edge_sum(padded_w, moved)

    def filter_block(block):
        previous = block.astype(jnp.float32)
        current = apply_op(previous)
        filtered = COEFFS[0] * previous + COEFFS[1] * current
        for order in range(2, DEGREE + 1):
            following = 2.0 * apply_op(current) - previous
            previous, current = (current, following)
            filtered = filtered + COEFFS[order] * following
        return filtered
    group = 16
    blocks = embeddings.reshape(NH, NW, C // group, group).transpose(2, 0, 1, 3)
    filtered = lax.map(filter_block, blocks).transpose(1, 2, 0, 3).reshape(NPIX, C)
    gram = jnp.dot(filtered.T.astype(jnp.float32), filtered.astype(jnp.float32), precision=lax.Precision.HIGHEST, preferred_element_type=jnp.float32)
    inverse = whitening(gram, NPIX)
    whitened = jnp.dot(filtered.astype(jnp.float32), inverse.astype(jnp.float32), precision=lax.Precision.HIGHEST, preferred_element_type=jnp.float32)
    labels = assignment.reshape(NPIX)
    sums = jax.ops.segment_sum(whitened, labels, num_segments=K)
    counts = jax.ops.segment_sum(jnp.ones((NPIX,), jnp.float32), labels, num_segments=K)
    centroids = sums / (counts + 1.0)[:, None]
    cent_norms = lax.optimization_barrier(jnp.sum(centroids * centroids, axis=1))

    def nearest(pixel_rows):
        cross = jnp.dot(pixel_rows.astype(jnp.float32), centroids.T.astype(jnp.float32), precision=lax.Precision.HIGHEST, preferred_element_type=jnp.float32)
        norms = lax.optimization_barrier(jnp.sum(pixel_rows * pixel_rows, axis=1))
        return lax.optimization_barrier(jnp.min((norms[:, None] - 2.0 * cross + cent_norms[None, :]) / C, axis=1))
    best = lax.map(nearest, whitened.reshape(NPIX // (TH * TW), TH * TW, C)).reshape(NH, NW)
    return (best, centroids)
```

```python
import functools
import math

import jax
import jax.numpy as jnp
from jax import lax
from jax.experimental import pallas as pl
from jax.experimental.pallas import tpu as pltpu
from jax.sharding import Mesh
from jax.sharding import PartitionSpec as P

K = 1024
C = 128
TH = 8
TW = 128
HALO = 4
COEFFS = (0.5, 0.45, 0.35, 0.25, 0.15)
PARTS = 32
BLOCK = 40
ROWS_OF = K // PARTS
F32 = jnp.float32
BF16 = jnp.bfloat16


def split3(x):
    high = x.astype(BF16)
    rest = x - high.astype(F32)
    mid = rest.astype(BF16)
    low = (rest - mid.astype(F32)).astype(BF16)
    return high, mid, low


def dot(a, b, dims):
    return lax.dot_general(a, b, (dims, ((), ())), preferred_element_type=F32)


def filter_kernel(
    xc_ref, xn_ref, xs_ref, xw_ref, xe_ref, wc_ref, ww_ref, we_ref, lab_ref,
    filt_ref, msg_ref, a_ref, b_ref, wb_ref, t_ref,
):
    zeros8 = jnp.zeros((16, 8, C), F32)
    for buf in (a_ref, b_ref):
        buf[:, 0:8, :] = zeros8
        buf[:, 152:160, :] = zeros8
    a_ref[:, 8:16, :] = xw_ref[...].astype(F32)
    a_ref[:, 144:152, :] = xe_ref[...].astype(F32)
    a_ref[0:4, 16:144, :] = xn_ref[...].astype(F32)
    a_ref[4:12, 16:144, :] = xc_ref[...].astype(F32)
    a_ref[12:16, 16:144, :] = xs_ref[...].astype(F32)

    lane = lax.broadcasted_iota(jnp.int32, (24, 128), 1)

    def weights(d):
        side = jnp.where(lane < 64, we_ref[d], ww_ref[d])
        return jnp.concatenate([wc_ref[d], side], axis=1)

    def right(x):
        return pltpu.roll(x, 255, 1)

    def left(x):
        return pltpu.roll(x, 1, 1)

    def down(x):
        return pltpu.roll(x, 23, 0)

    def up(x):
        return pltpu.roll(x, 1, 0)

    east, south, diag, anti = weights(0), weights(1), weights(2), weights(3)
    degree = east + left(east)
    degree = degree + south + up(south)
    degree = degree + diag + up(left(diag))
    degree = degree + anti + up(right(anti))
    scale = jnp.where(degree > 0.0, lax.rsqrt(jnp.where(degree > 0.0, degree, 1.0)), 0.0)
    below = down(scale)
    normed = (
        scale * east * right(scale),
        scale * south * below,
        scale * diag * right(below),
        scale * anti * left(below),
    )
    stack = jnp.concatenate(normed + (jnp.zeros((32, 256), F32),), axis=0)
    centre = stack[:, 0:128].T
    sides = stack[:, 128:256].T
    t_ref[0:8, :] = sides[120:128]
    t_ref[8:136, :] = centre
    t_ref[136:144, :] = sides[0:8]
    for d in range(4):
        for r in range(16):
            k = d * 24 + r + 4
            wb_ref[d, r, 0:8, :] = jnp.zeros((8, C), F32)
            wb_ref[d, r, 152:160, :] = jnp.zeros((8, C), F32)
            wb_ref[d, r, 8:152, :] = jnp.broadcast_to(t_ref[:, k:k + 1], (144, C))

    def apply_at(src, r, s, n):
        here, before, after = pl.ds(s, n), pl.ds(s - 1, n), pl.ds(s + 1, n)
        out = wb_ref[0, r, here, :] * src[r, after, :]
        out = out + wb_ref[0, r, before, :] * src[r, before, :]
        out = out + wb_ref[1, r, here, :] * src[r + 1, here, :]
        out = out + wb_ref[1, r - 1, here, :] * src[r - 1, here, :]
        out = out + wb_ref[2, r, here, :] * src[r + 1, after, :]
        out = out + wb_ref[2, r - 1, before, :] * src[r - 1, before, :]
        out = out + wb_ref[3, r, here, :] * src[r + 1, before, :]
        return out + wb_ref[3, r - 1, after, :] * src[r - 1, after, :]

    step = 24

    def first(r, carry):
        for s in range(8, 152, step):
            b_ref[r, s:s + step, :] = apply_at(a_ref, r, s, step)
        return carry

    def later(cur, prev):
        def body(r, carry):
            for s in range(8, 152, step):
                new = 2.0 * apply_at(cur, r, s, step) - prev[r, s:s + step, :]
                prev[r, s:s + step, :] = new
            return carry
        return body

    def accumulate(r, carry):
        for s in range(0, TW, 32):
            total = COEFFS[0] * a_ref[r + 4, 16 + s:48 + s, :] + COEFFS[1] * b_ref[r + 4, 16 + s:48 + s, :]
            filt_ref[pl.ds(r * TW + s, 32), :] = total
        return carry

    def add(src, coeff):
        def body(r, carry):
            for s in range(0, TW, 32):
                rows = pl.ds(r * TW + s, 32)
                filt_ref[rows, :] = filt_ref[rows, :] + coeff * src[r + 4, 16 + s:48 + s, :]
            return carry
        return body

    def last(r, carry):
        for s in range(0, TW, 16):
            here = pl.ds(s + 16, 16)
            new = 2.0 * apply_at(b_ref, r + 4, s + 16, 16) - a_ref[r + 4, here, :]
            rows = pl.ds(r * TW + s, 16)
            filt_ref[rows, :] = filt_ref[rows, :] + COEFFS[4] * new
        return carry

    lax.fori_loop(1, 15, first, 0)
    lax.fori_loop(0, TH, accumulate, 0)
    lax.fori_loop(2, 14, later(b_ref, a_ref), 0)
    lax.fori_loop(0, TH, add(a_ref, COEFFS[2]), 0)
    lax.fori_loop(3, 13, later(a_ref, b_ref), 0)
    lax.fori_loop(0, TH, add(b_ref, COEFFS[3]), 0)
    lax.fori_loop(0, TH, last, 0)

    high, mid, low = split3(filt_ref[...])
    tall = ((0,), (0,))
    by_high = dot(high, jnp.concatenate([high, mid, low], axis=1), tall)
    by_mid = dot(mid, jnp.concatenate([high, mid], axis=1), tall)
    by_low = dot(low, high, tall)
    gram = by_high[:, 2 * C:] + by_low + by_mid[:, C:]
    gram = gram + (by_high[:, C:2 * C] + by_mid[:, :C])
    gram = gram + by_high[:, :C]

    pieces = jnp.concatenate([high, mid, low], axis=1)
    ones = jnp.ones((8, TH * TW), BF16)
    chunk = 256
    for k0 in range(0, K, chunk):
        cluster = lax.broadcasted_iota(jnp.int32, (chunk, TW), 0) + k0
        onehot = jnp.concatenate(
            [(cluster == lab_ref[r:r + 1, :]).astype(F32).astype(BF16) for r in range(TH)], axis=1
        )
        part = dot(onehot, pieces, ((1,), (0,)))
        part = (part[:, 2 * C:] + part[:, C:2 * C]) + part[:, :C]
        counts = dot(ones, onehot, ((1,), (1,)))
        for q in range(chunk // ROWS_OF):
            p = k0 // ROWS_OF + q
            msg_ref[p, 0:ROWS_OF, :] = part[q * ROWS_OF:(q + 1) * ROWS_OF]
            msg_ref[p, ROWS_OF:ROWS_OF + 4, :] = gram[4 * p:4 * p + 4]
            lanes = (p * ROWS_OF - k0) // TW * TW
            msg_ref[p, ROWS_OF + 4:BLOCK, :] = counts[0:4, lanes:lanes + TW]


def run_filter(xc, xn, xs, xw, xe, wc, ww, we, labels):
    return pl.pallas_call(
        filter_kernel,
        out_shape=(
            jax.ShapeDtypeStruct((TH * TW, C), F32),
            jax.ShapeDtypeStruct((PARTS, BLOCK, C), F32),
        ),
        scratch_shapes=[
            pltpu.VMEM((16, 160, C), F32),
            pltpu.VMEM((16, 160, C), F32),
            pltpu.VMEM((4, 16, 160, C), F32),
            pltpu.VMEM((144, 128), F32),
        ],
        compiler_params=pltpu.CompilerParams(vmem_limit_bytes=40 * 2**20),
    )(xc, xn, xs, xw, xe, wc, ww, we, labels)


def finish_kernel(msg_ref, filt_ref, best_ref, cent_ref, g_ref, *, total):
    for p in range(PARTS):
        g_ref[4 * p:4 * p + 4, 0:C] = msg_ref[p, ROWS_OF:ROWS_OF + 4, :]
    row = lax.broadcasted_iota(jnp.int32, (C, C), 0)
    col = lax.broadcasted_iota(jnp.int32, (C, C), 1)
    g_ref[:, C:2 * C] = jnp.where(row == col, 1.0, 0.0).astype(F32)

    panel = 32
    sub = lax.broadcasted_iota(jnp.int32, (panel, 1), 0)
    for p0 in range(0, C, panel):
        left = g_ref[p0:p0 + panel, 0:C]
        right = g_ref[p0:p0 + panel, C:2 * C]
        for i in range(panel):
            j = p0 + i
            column = left[:, j:j + 1]
            pivot = left[i:i + 1, j:j + 1]
            root = lax.rsqrt(pivot)
            urow = left[i:i + 1, :] * root
            irow = right[i:i + 1, :] * root
            factor = jnp.where(sub > i, column * root, 0.0)
            keep = sub == i
            left = jnp.where(keep, urow, left - factor * urow)
            right = jnp.where(keep, irow, right - factor * irow)
        g_ref[p0:p0 + panel, 0:C] = left
        g_ref[p0:p0 + panel, C:2 * C] = right
        if p0 + panel < C:
            uh, um, ul = split3(left)
            full = jnp.concatenate([left, right], axis=1)
            fh, fm, fl = split3(full)
            lhs = jnp.concatenate([uh, um, ul, um, uh, uh], axis=0)
            rhs = jnp.concatenate([fl, fm, fh, fh, fm, fh], axis=0)
            update = dot(lhs, rhs, ((0,), (0,)))
            rest = slice(p0 + panel, C)
            g_ref[rest, :] = g_ref[rest, :] - update[p0 + panel:C, :]

    inverse = g_ref[:, C:2 * C] * math.sqrt(total)
    ih, im, il = split3(inverse)
    lhs = jnp.concatenate([il, im, ih, im, ih, ih], axis=1)

    def times_inverse(x, transposed):
        xh, xm, xl = split3(x)
        rhs = jnp.concatenate([xh, xm, xl, xh, xm, xh], axis=1)
        if transposed:
            return dot(lhs, rhs, ((1,), (1,)))
        return dot(rhs, lhs, ((1,), (1,)))

    whitened_t = times_inverse(filt_ref[...], True)
    norms = jnp.sum(whitened_t * whitened_t, axis=0, keepdims=True)
    wh, wm, wl = split3(whitened_t)
    w_all = jnp.concatenate([wl, wm, wh, wm, wh, wh], axis=0)
    best = None
    for b in range(K // C):
        sums = jnp.concatenate([msg_ref[4 * b + q, 0:ROWS_OF, :] for q in range(4)], axis=0)
        counts = jnp.broadcast_to(msg_ref[4 * b, ROWS_OF + 4:ROWS_OF + 5, :], (C, C)).T
        cent = times_inverse(sums, False) / (counts + 1.0)
        cent_ref[b * C:(b + 1) * C, :] = cent
        cent_norm = jnp.sum(cent * cent, axis=1, keepdims=True)
        ch, cm, cl = split3(-2.0 * cent)
        c_all = jnp.concatenate([ch, cm, cl, ch, cm, ch], axis=1)
        value = dot(c_all, w_all, ((1,), (0,))) + cent_norm
        low = jnp.min(value, axis=0, keepdims=True)
        best = low if best is None else jnp.minimum(best, low)
    result = (norms + best) / C
    for r in range(TH):
        best_ref[r:r + 1, :] = result[:, r * TW:(r + 1) * TW]


def run_finish(msg, filt, total):

    return pl.pallas_call(
        functools.partial(finish_kernel, total=total),
        out_shape=(
            jax.ShapeDtypeStruct((TH, TW), F32),
            jax.ShapeDtypeStruct((K, C), F32),
        ),
        scratch_shapes=[pltpu.VMEM((C, 2 * C), F32)],
        compiler_params=pltpu.CompilerParams(vmem_limit_bytes=40 * 2**20),
    )(msg, filt)


GY = ("xh", "y", "c")
GX = ("zh", "zl", "xl")


def shift(block, axes, size, forward):
    pairs = [(i, i + 1) for i in range(size - 1)]
    if not forward:
        pairs = [(b, a) for a, b in pairs]
    return lax.ppermute(block, axes, pairs)


def exchange(x, axes):
    return lax.all_to_all(x, axes, 0, 0)


def spread(x, axes, count):
    return exchange(jnp.broadcast_to(x[None], (count,) + x.shape), axes)


def reduce_all(msg):
    msg = jnp.sum(exchange(msg.reshape(2, PARTS // 2, BLOCK, C), "c"), axis=0)
    piece = jnp.sum(exchange(msg, ("xh", "y", "xl")), axis=0)
    piece = jnp.sum(spread(piece, "zl", 4), axis=0)
    piece = jnp.sum(spread(piece, "zh", 4), axis=0)
    half = spread(piece, ("xh", "y", "xl"), PARTS // 2)
    return lax.all_gather(half, "c", axis=0, tiled=True)


def on_device(embeddings, affinity, assignment):
    n_gy, n_gx = 16, 32
    xn = shift(embeddings[TH - HALO:], GY, n_gy, True)
    xs = shift(embeddings[:HALO], GY, n_gy, False)
    wn = shift(affinity, GY, n_gy, True)
    ws = shift(affinity, GY, n_gy, False)
    edge = jnp.concatenate([xn[:, TW - 8:], embeddings[:, TW - 8:], xs[:, TW - 8:]], axis=0)
    xw = shift(edge, GX, n_gx, True)
    edge = jnp.concatenate([xn[:, :8], embeddings[:, :8], xs[:, :8]], axis=0)
    xe = shift(edge, GX, n_gx, False)
    wc = jnp.concatenate([wn, affinity, ws], axis=1)
    ww = shift(wc, GX, n_gx, True)
    we = shift(wc, GX, n_gx, False)
    filt, msg = run_filter(embeddings, xn, xs, xw, xe, wc, ww, we, assignment)
    msg = reduce_all(msg)
    return run_finish(msg, filt, TH * TW * n_gy * n_gx)


def solution(mesh):
    inner = Mesh(mesh.devices.reshape(2, 4, 2, 4, 4, 2), GY + GX)
    return jax.shard_map(
        on_device,
        mesh=inner,
        in_specs=(P(GY, GX, None), P(None, GY, GX), P(GY, GX)),
        out_specs=(P(GY, GX), P()),
        check_vma=False,
    )
```

```python
import functools
import math

import jax
import jax.numpy as jnp
from jax import lax
from jax.experimental import pallas as pl
from jax.experimental.pallas import tpu as pltpu
from jax.sharding import Mesh
from jax.sharding import PartitionSpec as P

K = 1024
C = 128
TH = 8
TW = 128
HALO = 4
COEFFS = (0.5, 0.45, 0.35, 0.25, 0.15)
PARTS = 32
BLOCK = 40
ROWS_OF = K // PARTS
F32 = jnp.float32
BF16 = jnp.bfloat16


def split3(x):
    high = x.astype(BF16)
    rest = x - high.astype(F32)
    mid = rest.astype(BF16)
    low = (rest - mid.astype(F32)).astype(BF16)
    return high, mid, low


def dot(a, b, dims):
    return lax.dot_general(a, b, (dims, ((), ())), preferred_element_type=F32)


ROW_PIXELS = HALO * TW
ROW_MSG = ROW_PIXELS + 3 * 32
COL_PIXELS = 16 * 8
COL_MSG = COL_PIXELS + 3 * 96


def joined(ref, first, count):
    high, mid, low = (
        ref[first + q * count:first + (q + 1) * count, :].astype(F32) for q in range(3)
    )
    return (high + mid) + low


def pack_rows_kernel(odd_ref, x_ref, w_ref, near_ref, far_ref):
    planes = jnp.concatenate(split3(w_ref[...].reshape(32, TW)), axis=0)
    odd = odd_ref[0]
    top, bottom = 0, TH - HALO
    for ref, first in (
        (near_ref, jnp.where(odd == 1, top, bottom)), (far_ref, jnp.where(odd == 1, bottom, top))
    ):
        ref[0:ROW_PIXELS, :] = x_ref[pl.ds(first, HALO)].reshape(ROW_PIXELS, C)
        ref[ROW_PIXELS:ROW_MSG, :] = planes


def pack_cols_kernel(odd_ref, x_ref, w_ref, row_near_ref, row_far_ref, near_ref, far_ref, wide_ref, lo_ref, hi_ref):
    odd_row = odd_ref[0] == 1
    near_at = jnp.where(odd_row, 0, 1)
    for ref, at in ((row_near_ref, near_at), (row_far_ref, 1 - near_at)):
        weights = joined(ref, ROW_PIXELS, 32)
        for d in range(4):
            wide_ref[d, pl.ds(pl.multiple_of(16 * at, 8), 8), :] = weights[8 * d:8 * d + 8]
        for r in range(HALO):
            lo_ref[12 * at + r] = ref[r * TW:r * TW + 16, :].astype(F32)[0:8]
            hi_ref[12 * at + r] = ref[r * TW + TW - 16:r * TW + TW, :].astype(F32)[8:16]
    for d in range(4):
        wide_ref[d, 8:16, :] = w_ref[d]
    for r in range(TH):
        lo_ref[HALO + r] = x_ref[r, 0:16, :].astype(F32)[0:8]
        hi_ref[HALO + r] = x_ref[r, TW - 16:TW, :].astype(F32)[8:16]
    planes = jnp.concatenate(split3(wide_ref[...].reshape(96, TW)), axis=0)
    odd_col = odd_ref[1] == 1
    low = lo_ref[...].reshape(COL_PIXELS, C)
    high = hi_ref[...].reshape(COL_PIXELS, C)
    near_ref[0:COL_PIXELS, :] = jnp.where(odd_col, low, high).astype(BF16)
    far_ref[0:COL_PIXELS, :] = jnp.where(odd_col, high, low).astype(BF16)
    near_ref[COL_PIXELS:COL_MSG, :] = planes
    far_ref[COL_PIXELS:COL_MSG, :] = planes


def filter_kernel(
    odd_ref, xc_ref, row_near_ref, row_far_ref, col_near_ref, col_far_ref, wide_ref, lab_ref,
    filt_ref, msg_ref, a_ref, b_ref, wb_ref, t_ref,
):
    zeros8 = jnp.zeros((16, 8, C), F32)
    for buf in (a_ref, b_ref):
        buf[:, 0:8, :] = zeros8
        buf[:, 152:160, :] = zeros8
    near_at = jnp.where(odd_ref[0] == 1, 0, 1)
    for ref, at in ((row_near_ref, near_at), (row_far_ref, 1 - near_at)):
        a_ref[pl.ds(12 * at, HALO), 16:144, :] = ref[0:ROW_PIXELS, :].astype(F32).reshape(HALO, TW, C)
    a_ref[4:12, 16:144, :] = xc_ref[...].astype(F32)
    odd_col = odd_ref[1] == 1
    near = col_near_ref[0:COL_PIXELS, :].astype(F32).reshape(16, 8, C)
    far = col_far_ref[0:COL_PIXELS, :].astype(F32).reshape(16, 8, C)
    a_ref[:, 8:16, :] = jnp.where(odd_col, near, far)
    a_ref[:, 144:152, :] = jnp.where(odd_col, far, near)

    lane = lax.broadcasted_iota(jnp.int32, (96, TW), 1)
    near = joined(col_near_ref, COL_PIXELS, 96)
    far = joined(col_far_ref, COL_PIXELS, 96)
    sides = jnp.where((lane < 64) != odd_col, near, far)

    def weights(d):
        return jnp.concatenate([wide_ref[d], sides[24 * d:24 * d + 24]], axis=1)

    def right(x):
        return pltpu.roll(x, 255, 1)

    def left(x):
        return pltpu.roll(x, 1, 1)

    def down(x):
        return pltpu.roll(x, 23, 0)

    def up(x):
        return pltpu.roll(x, 1, 0)

    east, south, diag, anti = weights(0), weights(1), weights(2), weights(3)
    degree = east + left(east)
    degree = degree + south + up(south)
    degree = degree + diag + up(left(diag))
    degree = degree + anti + up(right(anti))
    scale = jnp.where(degree > 0.0, lax.rsqrt(jnp.where(degree > 0.0, degree, 1.0)), 0.0)
    below = down(scale)
    normed = (
        scale * east * right(scale),
        scale * south * below,
        scale * diag * right(below),
        scale * anti * left(below),
    )
    stack = jnp.concatenate(normed + (jnp.zeros((32, 256), F32),), axis=0)
    centre = stack[:, 0:128].T
    sides = stack[:, 128:256].T
    t_ref[0:8, :] = sides[120:128]
    t_ref[8:136, :] = centre
    t_ref[136:144, :] = sides[0:8]
    for d in range(4):
        for r in range(16):
            k = d * 24 + r + 4
            wb_ref[d, r, 0:8, :] = jnp.zeros((8, C), F32)
            wb_ref[d, r, 152:160, :] = jnp.zeros((8, C), F32)
            wb_ref[d, r, 8:152, :] = jnp.broadcast_to(t_ref[:, k:k + 1], (144, C))

    def apply_at(src, r, s, n):
        here, before, after = pl.ds(s, n), pl.ds(s - 1, n), pl.ds(s + 1, n)
        out = wb_ref[0, r, here, :] * src[r, after, :]
        out = out + wb_ref[0, r, before, :] * src[r, before, :]
        out = out + wb_ref[1, r, here, :] * src[r + 1, here, :]
        out = out + wb_ref[1, r - 1, here, :] * src[r - 1, here, :]
        out = out + wb_ref[2, r, here, :] * src[r + 1, after, :]
        out = out + wb_ref[2, r - 1, before, :] * src[r - 1, before, :]
        out = out + wb_ref[3, r, here, :] * src[r + 1, before, :]
        return out + wb_ref[3, r - 1, after, :] * src[r - 1, after, :]

    step = 24

    def first(r, carry):
        for s in range(8, 152, step):
            b_ref[r, s:s + step, :] = apply_at(a_ref, r, s, step)
        return carry

    def later(cur, prev):
        def body(r, carry):
            for s in range(8, 152, step):
                new = 2.0 * apply_at(cur, r, s, step) - prev[r, s:s + step, :]
                prev[r, s:s + step, :] = new
            return carry
        return body

    def accumulate(r, carry):
        for s in range(0, TW, 32):
            total = COEFFS[0] * a_ref[r + 4, 16 + s:48 + s, :] + COEFFS[1] * b_ref[r + 4, 16 + s:48 + s, :]
            filt_ref[pl.ds(r * TW + s, 32), :] = total
        return carry

    def add(src, coeff):
        def body(r, carry):
            for s in range(0, TW, 32):
                rows = pl.ds(r * TW + s, 32)
                filt_ref[rows, :] = filt_ref[rows, :] + coeff * src[r + 4, 16 + s:48 + s, :]
            return carry
        return body

    def last(r, carry):
        for s in range(0, TW, 16):
            here = pl.ds(s + 16, 16)
            new = 2.0 * apply_at(b_ref, r + 4, s + 16, 16) - a_ref[r + 4, here, :]
            rows = pl.ds(r * TW + s, 16)
            filt_ref[rows, :] = filt_ref[rows, :] + COEFFS[4] * new
        return carry

    lax.fori_loop(1, 15, first, 0)
    lax.fori_loop(0, TH, accumulate, 0)
    lax.fori_loop(2, 14, later(b_ref, a_ref), 0)
    lax.fori_loop(0, TH, add(a_ref, COEFFS[2]), 0)
    lax.fori_loop(3, 13, later(a_ref, b_ref), 0)
    lax.fori_loop(0, TH, add(b_ref, COEFFS[3]), 0)
    lax.fori_loop(0, TH, last, 0)

    high, mid, low = split3(filt_ref[...])
    tall = ((0,), (0,))
    by_high = dot(high, jnp.concatenate([high, mid, low], axis=1), tall)
    by_mid = dot(mid, jnp.concatenate([high, mid], axis=1), tall)
    by_low = dot(low, high, tall)
    gram = by_high[:, 2 * C:] + by_low + by_mid[:, C:]
    gram = gram + (by_high[:, C:2 * C] + by_mid[:, :C])
    gram = gram + by_high[:, :C]

    pieces = jnp.concatenate([high, mid, low], axis=1)
    ones = jnp.ones((8, TH * TW), BF16)
    chunk = 256
    for k0 in range(0, K, chunk):
        cluster = lax.broadcasted_iota(jnp.int32, (chunk, TW), 0) + k0
        onehot = jnp.concatenate(
            [(cluster == lab_ref[r:r + 1, :]).astype(F32).astype(BF16) for r in range(TH)], axis=1
        )
        part = dot(onehot, pieces, ((1,), (0,)))
        part = (part[:, 2 * C:] + part[:, C:2 * C]) + part[:, :C]
        counts = dot(ones, onehot, ((1,), (1,)))
        for q in range(chunk // ROWS_OF):
            p = k0 // ROWS_OF + q
            msg_ref[p, 0:ROWS_OF, :] = part[q * ROWS_OF:(q + 1) * ROWS_OF]
            msg_ref[p, ROWS_OF:ROWS_OF + 4, :] = gram[4 * p:4 * p + 4]
            lanes = (p * ROWS_OF - k0) // TW * TW
            msg_ref[p, ROWS_OF + 4:BLOCK, :] = counts[0:4, lanes:lanes + TW]


SCALARS = pl.BlockSpec(memory_space=pltpu.SMEM)
VECTORS = pl.BlockSpec(memory_space=pltpu.VMEM)


def pack_rows(odd, x, w):
    shape = jax.ShapeDtypeStruct((ROW_MSG, C), BF16)
    return pl.pallas_call(
        pack_rows_kernel,
        out_shape=(shape, shape),
        in_specs=[SCALARS, VECTORS, VECTORS],
        compiler_params=pltpu.CompilerParams(vmem_limit_bytes=8 * 2**20),
    )(odd, x, w)


def pack_cols(odd, x, w, near, far):
    shape = jax.ShapeDtypeStruct((COL_MSG, C), BF16)
    wide = jax.ShapeDtypeStruct((4, 24, TW), F32)
    return pl.pallas_call(
        pack_cols_kernel,
        out_shape=(shape, shape, wide),
        in_specs=[SCALARS] + [VECTORS] * 4,
        scratch_shapes=[pltpu.VMEM((16, 8, C), F32)] * 2,
        compiler_params=pltpu.CompilerParams(vmem_limit_bytes=8 * 2**20),
    )(odd, x, w, near, far)


def run_filter(*args):
    return pl.pallas_call(
        filter_kernel,
        in_specs=[SCALARS] + [VECTORS] * 7,
        out_shape=(
            jax.ShapeDtypeStruct((TH * TW, C), F32),
            jax.ShapeDtypeStruct((PARTS, BLOCK, C), F32),
        ),
        scratch_shapes=[
            pltpu.VMEM((16, 160, C), F32),
            pltpu.VMEM((16, 160, C), F32),
            pltpu.VMEM((4, 16, 160, C), F32),
            pltpu.VMEM((144, 128), F32),
        ],
        compiler_params=pltpu.CompilerParams(vmem_limit_bytes=32 * 2**20),
    )(*args)


def eliminate(g_ref, panel=64, group=8):
    for p0 in range(0, C, panel):
        end = p0 + panel
        for i0 in range(p0, end, group):
            rows = end - i0
            left = g_ref[i0:end, 0:C]
            right = g_ref[i0:end, C:2 * C]
            sub = lax.broadcasted_iota(jnp.int32, (rows, C), 0)
            cols = [jnp.broadcast_to(left[:, i0 + k:i0 + k + 1], (rows, C)) for k in range(group)]
            lrow = [left[k:k + 1, :] for k in range(group)]
            rrow = [right[k:k + 1, :] for k in range(group)]
            a = [[cols[m][k:k + 1, :] for m in range(group)] for k in range(group)]
            for k in range(group):
                root = lax.rsqrt(a[k][k])
                s = [a[k][m] * root for m in range(group)]
                lrow[k] = lrow[k] * root
                rrow[k] = rrow[k] * root
                cols[k] = cols[k] * root
                for m in range(k + 1, group):
                    for n in range(m, group):
                        a[m][n] = a[m][n] - s[m] * s[n]
                    lrow[m] = lrow[m] - s[m] * lrow[k]
                    rrow[m] = rrow[m] - s[m] * rrow[k]
                    cols[m] = cols[m] - s[m] * cols[k]
            if rows > group:
                for k in range(group):
                    factor = jnp.where(sub >= group, cols[k], 0.0)
                    left = left - factor * lrow[k]
                    right = right - factor * rrow[k]
            for k in range(group):
                left = jnp.where(sub == k, lrow[k], left)
                right = jnp.where(sub == k, rrow[k], right)
            g_ref[i0:end, 0:C] = left
            g_ref[i0:end, C:2 * C] = right
        if end < C:
            uh, um, ul = split3(g_ref[p0:end, 0:C])
            fh, fm, fl = split3(g_ref[p0:end, :])
            lhs = jnp.concatenate([uh, um, ul, um, uh, uh], axis=0)
            rhs = jnp.concatenate([fl, fm, fh, fh, fm, fh], axis=0)
            update = dot(lhs, rhs, ((0,), (0,)))
            g_ref[end:C, :] = g_ref[end:C, :] - update[end:C, :]


def finish_kernel(msg_ref, filt_ref, best_ref, cent_ref, g_ref, *, total):
    for p in range(PARTS):
        g_ref[4 * p:4 * p + 4, 0:C] = msg_ref[p, ROWS_OF:ROWS_OF + 4, :]
    row = lax.broadcasted_iota(jnp.int32, (C, C), 0)
    col = lax.broadcasted_iota(jnp.int32, (C, C), 1)
    g_ref[:, C:2 * C] = jnp.where(row == col, 1.0, 0.0).astype(F32)

    eliminate(g_ref)
    inverse = g_ref[:, C:2 * C] * math.sqrt(total)
    ih, im, il = split3(inverse)
    lhs = jnp.concatenate([il, im, ih, im, ih, ih], axis=1)

    def times_inverse(x, transposed):
        xh, xm, xl = split3(x)
        rhs = jnp.concatenate([xh, xm, xl, xh, xm, xh], axis=1)
        if transposed:
            return dot(lhs, rhs, ((1,), (1,)))
        return dot(rhs, lhs, ((1,), (1,)))

    whitened_t = times_inverse(filt_ref[...], True)
    norms = jnp.sum(whitened_t * whitened_t, axis=0, keepdims=True)
    wh, wm, wl = split3(whitened_t)
    w_all = jnp.concatenate([wl, wm, wh, wm, wh, wh], axis=0)
    best = None
    for b in range(K // C):
        sums = jnp.concatenate([msg_ref[4 * b + q, 0:ROWS_OF, :] for q in range(4)], axis=0)
        counts = jnp.broadcast_to(msg_ref[4 * b, ROWS_OF + 4:ROWS_OF + 5, :], (C, C)).T
        cent = times_inverse(sums, False) / (counts + 1.0)
        cent_ref[b * C:(b + 1) * C, :] = cent
        cent_norm = jnp.sum(cent * cent, axis=1, keepdims=True)
        ch, cm, cl = split3(-2.0 * cent)
        c_all = jnp.concatenate([ch, cm, cl, ch, cm, ch], axis=1)
        value = dot(c_all, w_all, ((1,), (0,))) + cent_norm
        low = jnp.min(value, axis=0, keepdims=True)
        best = low if best is None else jnp.minimum(best, low)
    result = (norms + best) / C
    for r in range(TH):
        best_ref[r:r + 1, :] = result[:, r * TW:(r + 1) * TW]


def run_finish(msg, filt, total):

    return pl.pallas_call(
        functools.partial(finish_kernel, total=total),
        out_shape=(
            jax.ShapeDtypeStruct((TH, TW), F32),
            jax.ShapeDtypeStruct((K, C), F32),
        ),
        scratch_shapes=[pltpu.VMEM((C, 2 * C), F32)],
        compiler_params=pltpu.CompilerParams(vmem_limit_bytes=32 * 2**20),
    )(msg, filt)


GY = ("xh", "y", "c")
GX = ("zh", "zl", "xl")


def swap(near, far, axes, size):
    near_pairs = [(i, i ^ 1) for i in range(size)]
    far_pairs = [(i, i + 1) for i in range(1, size - 1, 2)]
    far_pairs = far_pairs + [(b, a) for a, b in far_pairs]
    far = lax.ppermute(far, axes, far_pairs)
    return lax.ppermute(near, axes, near_pairs), far


def exchange(x, axes):
    return lax.all_to_all(x, axes, 0, 0)


def spread(x, axes, count):
    return exchange(jnp.broadcast_to(x[None], (count,) + x.shape), axes)


def reduce_all(msg):
    piece = jnp.sum(exchange(msg, ("c", "xh", "y", "xl")), axis=0)
    piece = jnp.sum(spread(piece, "zl", 4), axis=0)
    piece = jnp.sum(spread(piece, "zh", 4), axis=0)
    half = spread(piece, ("xh", "y", "xl"), PARTS // 2)
    return lax.all_gather(half, "c", axis=0, tiled=True)


def on_device(embeddings, affinity, assignment):
    n_gy, n_gx = 16, 32
    odd = jnp.stack([lax.axis_index("c"), lax.axis_index("xl")]).astype(jnp.int32)
    rows = swap(*pack_rows(odd, embeddings, affinity), GY, n_gy)
    near, far, wide = pack_cols(odd, embeddings, affinity, *rows)
    cols = swap(near, far, GX, n_gx)
    filt, msg = run_filter(odd, embeddings, *rows, *cols, wide, assignment)
    msg = reduce_all(msg)
    return run_finish(msg, filt, TH * TW * n_gy * n_gx)


def solution(mesh):
    inner = Mesh(mesh.devices.reshape(2, 4, 2, 4, 4, 2), GY + GX)
    return jax.shard_map(
        on_device,
        mesh=inner,
        in_specs=(P(GY, GX, None), P(None, GY, GX), P(GY, GX)),
        out_specs=(P(GY, GX), P()),
        check_vma=False,
    )
```

```python
import functools
import math

import jax
import jax.numpy as jnp
from jax import lax
from jax.experimental import pallas as pl
from jax.experimental.pallas import tpu as pltpu
from jax.sharding import Mesh
from jax.sharding import PartitionSpec as P

K = 1024
C = 128
TH = 8
TW = 128
HALO = 4
DEGREE = 4
COEFFS = (0.5, 0.45, 0.35, 0.25, 0.15)
POWERS = (
    COEFFS[0] - COEFFS[2] + COEFFS[4],
    COEFFS[1] - 3.0 * COEFFS[3],
    2.0 * COEFFS[2] - 8.0 * COEFFS[4],
    4.0 * COEFFS[3],
    8.0 * COEFFS[4],
)
PARTS = 32
HOT = 256
BLOCK = 40
ROWS_OF = K // PARTS
F32 = jnp.float32
BF16 = jnp.bfloat16


def split3(x):
    high = x.astype(BF16)
    rest = x - high.astype(F32)
    mid = rest.astype(BF16)
    low = (rest - mid.astype(F32)).astype(BF16)
    return high, mid, low


def dot(a, b, dims):
    return lax.dot_general(a, b, (dims, ((), ())), preferred_element_type=F32)


ROW_PIXELS = HALO * TW
ROW_MSG = ROW_PIXELS + 3 * 32
COL_PIXELS = 16 * 8
COL_MSG = COL_PIXELS + 3 * 8


def joined(ref, first, count):
    pieces = ref[first:first + 3 * count, :].astype(F32)
    return (pieces[0:count] + pieces[count:2 * count]) + pieces[2 * count:]


def folded(x, first):
    lane = lax.broadcasted_iota(jnp.int32, (8, TW), 1) // 8
    out = jnp.zeros((8, TW), F32)
    for v in range(12):
        moved = pltpu.roll(x[8 * v:8 * v + 8], (8 * v - first) % TW, 1)
        out = jnp.where(lane == v, moved, out)
    return out


def unfolded(low, high):
    lane = lax.broadcasted_iota(jnp.int32, (8, TW), 1)
    return jnp.concatenate(
        [
            jnp.where(
                lane < 64,
                pltpu.roll(low, -8 * v % TW, 1),
                pltpu.roll(high, (TW - 8 - 8 * v) % TW, 1),
            )
            for v in range(12)
        ],
        axis=0,
    )


def pack_rows_kernel(odd_ref, x_ref, w_ref, near_ref, far_ref):
    planes = jnp.concatenate(split3(w_ref[...].reshape(32, TW)), axis=0)
    odd = odd_ref[0]
    for ref, first in ((near_ref, 1 - odd), (far_ref, odd)):
        pixels = pl.ds(pl.multiple_of(first * ROW_PIXELS, ROW_PIXELS), ROW_PIXELS)
        ref[0:ROW_PIXELS, :] = x_ref[pixels, :]
        ref[ROW_PIXELS:ROW_MSG, :] = planes


def pack_cols_kernel(
    odd_ref, x_ref, w_ref, row_near_ref, row_far_ref,
    near_ref, far_ref, wide_ref, x_out_ref, lo_ref, hi_ref,
):
    x_out_ref[...] = x_ref[...]
    odd_row = odd_ref[0] == 1
    near_at = jnp.where(odd_row, 0, 1)
    for ref, at in ((row_near_ref, near_at), (row_far_ref, 1 - near_at)):
        weights = joined(ref, ROW_PIXELS, 32)
        for d in range(4):
            wide_ref[d, pl.ds(pl.multiple_of(16 * at, 8), 8), :] = weights[8 * d:8 * d + 8]
        for r in range(HALO):
            lo_ref[12 * at + r] = ref[r * TW:r * TW + 16, :].astype(F32)[0:8]
            hi_ref[12 * at + r] = ref[r * TW + TW - 16:r * TW + TW, :].astype(F32)[8:16]
    for d in range(4):
        wide_ref[d, 8:16, :] = w_ref[d]
    for r in range(TH):
        lo_ref[HALO + r] = x_ref[r * TW:r * TW + 16, :].astype(F32)[0:8]
        hi_ref[HALO + r] = x_ref[r * TW + TW - 16:r * TW + TW, :].astype(F32)[8:16]
    odd_col = odd_ref[1] == 1
    wide = wide_ref[...].reshape(96, TW)
    low, high = folded(wide, 0), folded(wide, TW - 8)
    for ref, part in (
        (near_ref, jnp.where(odd_col, low, high)), (far_ref, jnp.where(odd_col, high, low))
    ):
        ref[COL_PIXELS:COL_MSG, :] = jnp.concatenate([q.astype(F32) for q in split3(part)], axis=0).astype(BF16)
    low = lo_ref[...].reshape(COL_PIXELS, C)
    high = hi_ref[...].reshape(COL_PIXELS, C)
    near_ref[0:COL_PIXELS, :] = jnp.where(odd_col, low, high).astype(BF16)
    far_ref[0:COL_PIXELS, :] = jnp.where(odd_col, high, low).astype(BF16)


def normed_weights(wide_ref, sides):
    def weights(d):
        return jnp.concatenate([wide_ref[d], sides[24 * d:24 * d + 24]], axis=1)

    def right(x):
        return pltpu.roll(x, 255, 1)

    def left(x):
        return pltpu.roll(x, 1, 1)

    def down(x):
        return pltpu.roll(x, 23, 0)

    def up(x):
        return pltpu.roll(x, 1, 0)

    east, south, diag, anti = weights(0), weights(1), weights(2), weights(3)
    degree = east + left(east)
    degree = degree + south + up(south)
    degree = degree + diag + up(left(diag))
    degree = degree + anti + up(right(anti))
    scale = jnp.where(degree > 0.0, lax.rsqrt(jnp.where(degree > 0.0, degree, 1.0)), 0.0)
    below = down(scale)
    normed = (
        scale * east * right(scale),
        scale * south * below,
        scale * diag * right(below),
        scale * anti * left(below),
    )
    return jnp.concatenate(normed + (jnp.zeros((32, 256), F32),), axis=0)


def spread_weights(wb_ref, columns, first):
    count = columns.shape[0]
    for d in range(4):
        for r in range(16):
            k = d * 24 + r + 4
            wb_ref[d, r, first:first + count, :] = jnp.broadcast_to(columns[:, k:k + 1], (count, C))


def apply_rows(wb_ref, src, r, rows, s):
    x, w = {}, {}

    def field(q, off):
        if (q, off) not in x:
            x[q, off] = src[r + q, s + off:s + off + 8, :]
        return x[q, off]

    def weight(d, q, off):
        if (d, q, off) not in w:
            w[d, q, off] = wb_ref[d, r + q, s + off:s + off + 8, :]
        return w[d, q, off]

    outs = []
    for q in range(rows):
        out = weight(0, q, 0) * field(q, 1) + weight(0, q, -1) * field(q, -1)
        out = out + weight(1, q - 1, 0) * field(q - 1, 0)
        out = out + weight(2, q - 1, -1) * field(q - 1, -1)
        out = out + weight(3, q - 1, 1) * field(q - 1, 1)
        out = out + weight(1, q, 0) * field(q + 1, 0)
        out = out + weight(2, q, 0) * field(q + 1, 1)
        outs.append(out + weight(3, q, 0) * field(q + 1, -1))
    return outs


def sweep(step, tiles, wb_ref, start_ref, src, dst):
    rows = (16 - 2 * step) // 2
    for r in (step, step + rows):
        for t in tiles:
            s = 8 + 8 * t
            for q, new in enumerate(apply_rows(wb_ref, src, r, rows, s)):
                start = start_ref[r + q, s:s + 8, :]
                if step == 1:
                    new = POWERS[4] * new + POWERS[3] * start
                else:
                    new = new + POWERS[DEGREE - step] * start
                if step < DEGREE:
                    dst[r + q, s:s + 8, :] = new
                else:
                    pixel = (r + q - 4) * TW + s - 16
                    dst[pixel:pixel + 8, :] = new


def prepare_kernel(
    odd_ref, x_ref, row_near_ref, row_far_ref, wide_ref, lab_ref,
    hot_ref, count_ref, a_ref, b_ref, c_ref, filt_ref, wb_ref,
):
    zeros8 = jnp.zeros((16, 8, C), F32)
    for buf in (a_ref, b_ref, c_ref, wb_ref.at[0], wb_ref.at[1], wb_ref.at[2], wb_ref.at[3]):
        buf[:, 0:8, :] = zeros8
        buf[:, 152:160, :] = zeros8
    near_at = jnp.where(odd_ref[0] == 1, 0, 1)
    for ref, at in ((row_near_ref, near_at), (row_far_ref, 1 - near_at)):
        a_ref[pl.ds(12 * at, HALO), 16:144, :] = ref[0:ROW_PIXELS, :].astype(F32).reshape(HALO, TW, C)
    a_ref[4:12, 16:144, :] = x_ref[...].astype(F32).reshape(TH, TW, C)
    stack = normed_weights(wide_ref, jnp.zeros((96, TW), F32))
    spread_weights(wb_ref, stack[:, 0:TW].T[8:120], 24)
    sweep(1, range(3, 15), wb_ref, a_ref, a_ref, b_ref)
    sweep(2, range(4, 14), wb_ref, a_ref, b_ref, c_ref)
    sweep(3, range(5, 13), wb_ref, a_ref, c_ref, b_ref)
    sweep(4, range(6, 12), wb_ref, a_ref, b_ref, filt_ref)
    ones = jnp.ones((8, TH * TW), BF16)
    for k0 in range(0, K, HOT):
        cluster = lax.broadcasted_iota(jnp.int32, (HOT, TW), 0) + k0
        onehot = jnp.concatenate(
            [(cluster == lab_ref[r:r + 1, :]).astype(F32).astype(BF16) for r in range(TH)], axis=1
        )
        hot_ref[k0:k0 + HOT, :] = onehot
        count_ref[:, k0:k0 + HOT] = dot(ones, onehot, ((1,), (1,)))


def filter_kernel(
    odd_ref, col_near_ref, col_far_ref, wide_ref, hot_ref, count_ref, *refs,
):
    a_ref, b_ref, c_ref, filt_ref, wb_ref, msg_ref = refs[5:]
    odd_col = odd_ref[1] == 1
    near = col_near_ref[0:COL_PIXELS, :].astype(F32).reshape(16, 8, C)
    far = col_far_ref[0:COL_PIXELS, :].astype(F32).reshape(16, 8, C)
    a_ref[:, 8:16, :] = jnp.where(odd_col, near, far)
    a_ref[:, 144:152, :] = jnp.where(odd_col, far, near)
    near = joined(col_near_ref, COL_PIXELS, 8)
    far = joined(col_far_ref, COL_PIXELS, 8)
    sides = unfolded(jnp.where(odd_col, far, near), jnp.where(odd_col, near, far))
    stack = normed_weights(wide_ref, sides)
    centre = stack[:, 0:TW].T
    sides = stack[:, TW:2 * TW].T
    spread_weights(wb_ref, jnp.concatenate([sides[120:128], centre[0:8]], axis=0), 8)
    spread_weights(wb_ref, jnp.concatenate([centre[120:128], sides[0:8]], axis=0), 136)
    sweep(1, (0, 1, 2, 15, 16, 17), wb_ref, a_ref, a_ref, b_ref)
    sweep(2, (0, 1, 2, 3, 14, 15, 16, 17), wb_ref, a_ref, b_ref, c_ref)
    sweep(3, (0, 1, 2, 3, 4, 13, 14, 15, 16, 17), wb_ref, a_ref, c_ref, b_ref)
    sweep(4, (1, 2, 3, 4, 5, 12, 13, 14, 15, 16), wb_ref, a_ref, b_ref, filt_ref)

    high, mid, low = split3(filt_ref[...])
    tall = ((0,), (0,))
    by_high = dot(high, jnp.concatenate([high, mid, low], axis=1), tall)
    by_mid = dot(mid, jnp.concatenate([high, mid], axis=1), tall)
    by_low = dot(low, high, tall)
    gram = by_high[:, 2 * C:] + by_low + by_mid[:, C:]
    gram = gram + (by_high[:, C:2 * C] + by_mid[:, :C])
    gram = gram + by_high[:, :C]

    pieces = jnp.concatenate([high, mid, low], axis=1)
    for k0 in range(0, K, HOT):
        part = dot(hot_ref[k0:k0 + HOT, :], pieces, ((1,), (0,)))
        part = (part[:, 2 * C:] + part[:, C:2 * C]) + part[:, :C]
        for q in range(HOT // ROWS_OF):
            p = k0 // ROWS_OF + q
            msg_ref[p, 0:ROWS_OF, :] = part[q * ROWS_OF:(q + 1) * ROWS_OF]
            msg_ref[p, ROWS_OF:ROWS_OF + 4, :] = gram[4 * p:4 * p + 4]
            lanes = p * ROWS_OF // TW * TW
            msg_ref[p, ROWS_OF + 4:BLOCK, :] = count_ref[0:4, lanes:lanes + TW]


SCALARS = pl.BlockSpec(memory_space=pltpu.SMEM)
VECTORS = pl.BlockSpec(memory_space=pltpu.VMEM)


def pack_rows(odd, x, w):
    shape = jax.ShapeDtypeStruct((ROW_MSG, C), BF16)
    return pl.pallas_call(
        pack_rows_kernel,
        out_shape=(shape, shape),
        in_specs=[SCALARS] + [VECTORS] * 2,
        out_specs=(VECTORS,) * 2,
        compiler_params=pltpu.CompilerParams(vmem_limit_bytes=8 * 2**20),
    )(odd, x.reshape(TH * TW, C), w)


def pack_cols(odd, x, w, near, far):
    shape = jax.ShapeDtypeStruct((COL_MSG, C), BF16)
    return pl.pallas_call(
        pack_cols_kernel,
        out_shape=(
            shape,
            shape,
            jax.ShapeDtypeStruct((4, 24, TW), F32),
            jax.ShapeDtypeStruct((TH * TW, C), BF16),
        ),
        in_specs=[SCALARS] + [VECTORS] * 4,
        out_specs=(VECTORS,) * 4,
        scratch_shapes=[pltpu.VMEM((16, 8, C), F32)] * 2,
        compiler_params=pltpu.CompilerParams(vmem_limit_bytes=8 * 2**20),
    )(odd, x.reshape(TH * TW, C), w, near, far)


FIELD = jax.ShapeDtypeStruct((16, 160, C), F32)
BUFFERS = (
    FIELD,
    FIELD,
    FIELD,
    jax.ShapeDtypeStruct((TH * TW, C), F32),
    jax.ShapeDtypeStruct((4, 16, 160, C), F32),
)


def run_prepare(odd, x, near, far, wide, labels):
    outs = (
        jax.ShapeDtypeStruct((K, TH * TW), BF16),
        jax.ShapeDtypeStruct((8, K), F32),
    ) + BUFFERS
    return pl.pallas_call(
        prepare_kernel,
        out_shape=outs,
        in_specs=[SCALARS] + [VECTORS] * 5,
        out_specs=(VECTORS,) * 7,
        compiler_params=pltpu.CompilerParams(vmem_limit_bytes=16 * 2**20),
        cost_estimate=pl.CostEstimate(flops=2**27, bytes_accessed=2**23, transcendentals=0),
    )(odd, x, near, far, wide, labels)


def run_filter(odd, near, far, wide, hot, counts, *buffers):
    *_, filt, _, msg = pl.pallas_call(
        filter_kernel,
        in_specs=[SCALARS] + [VECTORS] * 10,
        out_shape=BUFFERS + (jax.ShapeDtypeStruct((PARTS, BLOCK, C), F32),),
        out_specs=(VECTORS,) * 6,
        input_output_aliases={6 + q: q for q in range(5)},
        compiler_params=pltpu.CompilerParams(vmem_limit_bytes=16 * 2**20),
    )(odd, near, far, wide, hot, counts, *buffers)
    return filt, msg


def eliminate(g_ref, panel=64, group=8):
    for p0 in range(0, C, panel):
        end = p0 + panel
        for i0 in range(p0, end, group):
            rows = end - i0
            left = g_ref[i0:end, 0:C]
            right = g_ref[i0:end, C:2 * C]
            sub = lax.broadcasted_iota(jnp.int32, (rows, C), 0)
            cols = [jnp.broadcast_to(left[:, i0 + k:i0 + k + 1], (rows, C)) for k in range(group)]
            lrow = [left[k:k + 1, :] for k in range(group)]
            rrow = [right[k:k + 1, :] for k in range(group)]
            a = [[cols[m][k:k + 1, :] for m in range(group)] for k in range(group)]
            for k in range(group):
                root = lax.rsqrt(a[k][k])
                s = [a[k][m] * root for m in range(group)]
                lrow[k] = lrow[k] * root
                rrow[k] = rrow[k] * root
                cols[k] = cols[k] * root
                for m in range(k + 1, group):
                    for n in range(m, group):
                        a[m][n] = a[m][n] - s[m] * s[n]
                    lrow[m] = lrow[m] - s[m] * lrow[k]
                    rrow[m] = rrow[m] - s[m] * rrow[k]
                    cols[m] = cols[m] - s[m] * cols[k]
            if rows > group:
                for k in range(group):
                    factor = jnp.where(sub >= group, cols[k], 0.0)
                    left = left - factor * lrow[k]
                    right = right - factor * rrow[k]
            for k in range(group):
                left = jnp.where(sub == k, lrow[k], left)
                right = jnp.where(sub == k, rrow[k], right)
            g_ref[i0:end, 0:C] = left
            g_ref[i0:end, C:2 * C] = right
        if end < C:
            uh, um, ul = split3(g_ref[p0:end, 0:C])
            fh, fm, fl = split3(g_ref[p0:end, :])
            lhs = jnp.concatenate([uh, um, ul, um, uh, uh], axis=0)
            rhs = jnp.concatenate([fl, fm, fh, fh, fm, fh], axis=0)
            update = dot(lhs, rhs, ((0,), (0,)))
            g_ref[end:C, :] = g_ref[end:C, :] - update[end:C, :]


def finish_kernel(msg_ref, filt_ref, best_ref, cent_ref, g_ref, *, total):
    for p in range(PARTS):
        g_ref[4 * p:4 * p + 4, 0:C] = msg_ref[p, ROWS_OF:ROWS_OF + 4, :]
    row = lax.broadcasted_iota(jnp.int32, (C, C), 0)
    col = lax.broadcasted_iota(jnp.int32, (C, C), 1)
    g_ref[:, C:2 * C] = jnp.where(row == col, 1.0, 0.0).astype(F32)

    eliminate(g_ref)
    inverse = g_ref[:, C:2 * C] * math.sqrt(total)
    ih, im, il = split3(inverse)
    lhs = jnp.concatenate([il, im, ih, im, ih, ih], axis=1)

    def times_inverse(x, transposed):
        xh, xm, xl = split3(x)
        rhs = jnp.concatenate([xh, xm, xl, xh, xm, xh], axis=1)
        if transposed:
            return dot(lhs, rhs, ((1,), (1,)))
        return dot(rhs, lhs, ((1,), (1,)))

    whitened_t = times_inverse(filt_ref[...], True)
    norms = jnp.sum(whitened_t * whitened_t, axis=0, keepdims=True)
    wh, wm, wl = split3(whitened_t)
    w_all = jnp.concatenate([wl, wm, wh, wm, wh, wh], axis=0)
    best = None
    for b in range(K // C):
        sums = jnp.concatenate([msg_ref[4 * b + q, 0:ROWS_OF, :] for q in range(4)], axis=0)
        counts = jnp.broadcast_to(msg_ref[4 * b, ROWS_OF + 4:ROWS_OF + 5, :], (C, C)).T
        cent = times_inverse(sums, False) / (counts + 1.0)
        cent_ref[b * C:(b + 1) * C, :] = cent
        cent_norm = jnp.sum(cent * cent, axis=1, keepdims=True)
        ch, cm, cl = split3(-2.0 * cent)
        c_all = jnp.concatenate([ch, cm, cl, ch, cm, ch], axis=1)
        value = dot(c_all, w_all, ((1,), (0,))) + cent_norm
        low = jnp.min(value, axis=0, keepdims=True)
        best = low if best is None else jnp.minimum(best, low)
    result = (norms + best) / C
    for r in range(TH):
        best_ref[r:r + 1, :] = result[:, r * TW:(r + 1) * TW]


def run_finish(msg, filt, total):

    return pl.pallas_call(
        functools.partial(finish_kernel, total=total),
        out_shape=(
            jax.ShapeDtypeStruct((TH, TW), F32),
            jax.ShapeDtypeStruct((K, C), F32),
        ),
        scratch_shapes=[pltpu.VMEM((C, 2 * C), F32)],
        compiler_params=pltpu.CompilerParams(vmem_limit_bytes=32 * 2**20),
    )(msg, filt)


GY = ("xh", "y", "c")
GX = ("zh", "zl", "xl")


def swap(near, far, axes, size):
    near_pairs = [(i, i ^ 1) for i in range(size)]
    far_pairs = [(i, i + 1) for i in range(1, size - 1, 2)]
    far_pairs = far_pairs + [(b, a) for a, b in far_pairs]
    far = lax.ppermute(far, axes, far_pairs)
    return lax.ppermute(near, axes, near_pairs), far


def exchange(x, axes):
    return lax.all_to_all(x, axes, 0, 0)


def spread(x, axes, count):
    return exchange(jnp.broadcast_to(x[None], (count,) + x.shape), axes)


def reduce_all(msg):
    piece = jnp.sum(exchange(msg, ("c", "xh", "y", "xl")), axis=0)
    piece = jnp.sum(spread(piece, "zl", 4), axis=0)
    piece = jnp.sum(spread(piece, "zh", 4), axis=0)
    half = spread(piece, ("xh", "y", "xl"), PARTS // 2)
    return lax.all_gather(half, "c", axis=0, tiled=True)


def on_device(embeddings, affinity, assignment):
    n_gy, n_gx = 16, 32
    odd = jnp.stack([lax.axis_index("c"), lax.axis_index("xl")]).astype(jnp.int32)
    rows = swap(*pack_rows(odd, embeddings, affinity), GY, n_gy)
    near, far, wide, pixels = pack_cols(odd, embeddings, affinity, *rows)
    prepared = run_prepare(odd, pixels, *rows, wide, assignment)
    cols = swap(near, far, GX, n_gx)
    filt, msg = run_filter(odd, *cols, wide, *prepared)
    msg = reduce_all(msg)
    return run_finish(msg, filt, TH * TW * n_gy * n_gx)


def solution(mesh):
    inner = Mesh(mesh.devices.reshape(2, 4, 2, 4, 4, 2), GY + GX)
    return jax.shard_map(
        on_device,
        mesh=inner,
        in_specs=(P(GY, GX, None), P(None, GY, GX), P(GY, GX)),
        out_specs=(P(GY, GX), P()),
        check_vma=False,
    )
```

```python
import functools
import math

import jax
import jax.numpy as jnp
from jax import lax
from jax.experimental import pallas as pl
from jax.experimental.pallas import tpu as pltpu
from jax.sharding import Mesh
from jax.sharding import PartitionSpec as P

K = 1024
C = 128
TH = 8
TW = 128
HALO = 4
DEGREE = 4
COEFFS = (0.5, 0.45, 0.35, 0.25, 0.15)
POWERS = (
    COEFFS[0] - COEFFS[2] + COEFFS[4],
    COEFFS[1] - 3.0 * COEFFS[3],
    2.0 * COEFFS[2] - 8.0 * COEFFS[4],
    4.0 * COEFFS[3],
    8.0 * COEFFS[4],
)
PARTS = 32
HOT = 256
BLOCK = 40
ROWS_OF = K // PARTS
F32 = jnp.float32
BF16 = jnp.bfloat16


def split3(x):
    high = x.astype(BF16)
    rest = x - high.astype(F32)
    mid = rest.astype(BF16)
    low = (rest - mid.astype(F32)).astype(BF16)
    return high, mid, low


def dot(a, b, dims):
    return lax.dot_general(a, b, (dims, ((), ())), preferred_element_type=F32)


ROW_PIXELS = HALO * TW
ROW_MSG = ROW_PIXELS + 3 * 32
COL_PIXELS = 16 * 8
COL_MSG = COL_PIXELS + 3 * 8


def joined(ref, first, count):
    pieces = ref[first:first + 3 * count, :].astype(F32)
    return (pieces[0:count] + pieces[count:2 * count]) + pieces[2 * count:]


def folded(x, first):
    lane = lax.broadcasted_iota(jnp.int32, (8, TW), 1) // 8
    out = jnp.zeros((8, TW), F32)
    for v in range(12):
        moved = pltpu.roll(x[8 * v:8 * v + 8], (8 * v - first) % TW, 1)
        out = jnp.where(lane == v, moved, out)
    return out


def unfolded(low, high):
    lane = lax.broadcasted_iota(jnp.int32, (8, TW), 1)
    return jnp.concatenate(
        [
            jnp.where(
                lane < 64,
                pltpu.roll(low, -8 * v % TW, 1),
                pltpu.roll(high, (TW - 8 - 8 * v) % TW, 1),
            )
            for v in range(12)
        ],
        axis=0,
    )


def pack_rows_kernel(odd_ref, x_ref, w_ref, near_ref, far_ref):
    planes = jnp.concatenate(split3(w_ref[...].reshape(32, TW)), axis=0)
    odd = odd_ref[0]
    for ref, first in ((near_ref, 1 - odd), (far_ref, odd)):
        pixels = pl.ds(pl.multiple_of(first * ROW_PIXELS, ROW_PIXELS), ROW_PIXELS)
        ref[0:ROW_PIXELS, :] = x_ref[pixels, :]
        ref[ROW_PIXELS:ROW_MSG, :] = planes


def pack_cols_kernel(
    odd_ref, x_ref, w_ref, row_near_ref, row_far_ref,
    near_ref, far_ref, wide_ref, x_out_ref, lo_ref, hi_ref,
):
    x_out_ref[...] = x_ref[...]
    odd_row = odd_ref[0] == 1
    near_at = jnp.where(odd_row, 0, 1)
    for ref, at in ((row_near_ref, near_at), (row_far_ref, 1 - near_at)):
        weights = joined(ref, ROW_PIXELS, 32)
        for d in range(4):
            wide_ref[d, pl.ds(pl.multiple_of(16 * at, 8), 8), :] = weights[8 * d:8 * d + 8]
        for r in range(HALO):
            lo_ref[12 * at + r] = ref[r * TW:r * TW + 16, :].astype(F32)[0:8]
            hi_ref[12 * at + r] = ref[r * TW + TW - 16:r * TW + TW, :].astype(F32)[8:16]
    for d in range(4):
        wide_ref[d, 8:16, :] = w_ref[d]
    for r in range(TH):
        lo_ref[HALO + r] = x_ref[r * TW:r * TW + 16, :].astype(F32)[0:8]
        hi_ref[HALO + r] = x_ref[r * TW + TW - 16:r * TW + TW, :].astype(F32)[8:16]
    odd_col = odd_ref[1] == 1
    wide = wide_ref[...].reshape(96, TW)
    low, high = folded(wide, 0), folded(wide, TW - 8)
    for ref, part in (
        (near_ref, jnp.where(odd_col, low, high)), (far_ref, jnp.where(odd_col, high, low))
    ):
        ref[COL_PIXELS:COL_MSG, :] = jnp.concatenate([q.astype(F32) for q in split3(part)], axis=0).astype(BF16)
    low = lo_ref[...].reshape(COL_PIXELS, C)
    high = hi_ref[...].reshape(COL_PIXELS, C)
    near_ref[0:COL_PIXELS, :] = jnp.where(odd_col, low, high).astype(BF16)
    far_ref[0:COL_PIXELS, :] = jnp.where(odd_col, high, low).astype(BF16)


def normed_weights(wide_ref, sides):
    def weights(d):
        return jnp.concatenate([wide_ref[d], sides[24 * d:24 * d + 24]], axis=1)

    def right(x):
        return pltpu.roll(x, 255, 1)

    def left(x):
        return pltpu.roll(x, 1, 1)

    def down(x):
        return pltpu.roll(x, 23, 0)

    def up(x):
        return pltpu.roll(x, 1, 0)

    east, south, diag, anti = weights(0), weights(1), weights(2), weights(3)
    degree = east + left(east)
    degree = degree + south + up(south)
    degree = degree + diag + up(left(diag))
    degree = degree + anti + up(right(anti))
    scale = jnp.where(degree > 0.0, lax.rsqrt(jnp.where(degree > 0.0, degree, 1.0)), 0.0)
    below = down(scale)
    normed = (
        scale * east * right(scale),
        scale * south * below,
        scale * diag * right(below),
        scale * anti * left(below),
    )
    return jnp.concatenate(normed + (jnp.zeros((32, 256), F32),), axis=0)


def spread_weights(wb_ref, columns, first):
    count = columns.shape[0]
    for d in range(4):
        for r in range(16):
            k = d * 24 + r + 4
            wb_ref[d, r, first:first + count, :] = jnp.broadcast_to(columns[:, k:k + 1], (count, C))


def apply_rows(wb_ref, src, r, rows, s):
    x, w = {}, {}

    def field(q, off):
        if (q, off) not in x:
            x[q, off] = src[r + q, s + off:s + off + 8, :]
        return x[q, off]

    def weight(d, q, off):
        if (d, q, off) not in w:
            w[d, q, off] = wb_ref[d, r + q, s + off:s + off + 8, :]
        return w[d, q, off]

    outs = []
    for q in range(rows):
        out = weight(0, q, 0) * field(q, 1) + weight(0, q, -1) * field(q, -1)
        out = out + weight(1, q - 1, 0) * field(q - 1, 0)
        out = out + weight(2, q - 1, -1) * field(q - 1, -1)
        out = out + weight(3, q - 1, 1) * field(q - 1, 1)
        out = out + weight(1, q, 0) * field(q + 1, 0)
        out = out + weight(2, q, 0) * field(q + 1, 1)
        outs.append(out + weight(3, q, 0) * field(q + 1, -1))
    return outs


def sweep(step, tiles, wb_ref, start_ref, src, dst):
    rows = (16 - 2 * step) // 2
    for r in (step, step + rows):
        for t in tiles:
            s = 8 + 8 * t
            for q, new in enumerate(apply_rows(wb_ref, src, r, rows, s)):
                start = start_ref[r + q, s:s + 8, :]
                if step == 1:
                    new = POWERS[4] * new + POWERS[3] * start
                else:
                    new = new + POWERS[DEGREE - step] * start
                if step < DEGREE:
                    dst[r + q, s:s + 8, :] = new
                else:
                    pixel = (r + q - 4) * TW + s - 16
                    dst[pixel:pixel + 8, :] = new


def prepare_kernel(
    odd_ref, x_ref, row_near_ref, row_far_ref, wide_ref, lab_ref,
    hot_ref, count_ref, a_ref, b_ref, c_ref, filt_ref, wb_ref,
):
    zeros8 = jnp.zeros((16, 8, C), F32)
    for buf in (a_ref, b_ref, c_ref, wb_ref.at[0], wb_ref.at[1], wb_ref.at[2], wb_ref.at[3]):
        buf[:, 0:8, :] = zeros8
        buf[:, 152:160, :] = zeros8
    near_at = jnp.where(odd_ref[0] == 1, 0, 1)
    for ref, at in ((row_near_ref, near_at), (row_far_ref, 1 - near_at)):
        a_ref[pl.ds(12 * at, HALO), 16:144, :] = ref[0:ROW_PIXELS, :].astype(F32).reshape(HALO, TW, C)
    a_ref[4:12, 16:144, :] = x_ref[...].astype(F32).reshape(TH, TW, C)
    stack = normed_weights(wide_ref, jnp.zeros((96, TW), F32))
    spread_weights(wb_ref, stack[:, 0:TW].T[8:120], 24)
    sweep(1, range(3, 15), wb_ref, a_ref, a_ref, b_ref)
    sweep(2, range(4, 14), wb_ref, a_ref, b_ref, c_ref)
    sweep(3, range(5, 13), wb_ref, a_ref, c_ref, b_ref)
    sweep(4, range(6, 12), wb_ref, a_ref, b_ref, filt_ref)
    ones = jnp.ones((8, TH * TW), BF16)
    for k0 in range(0, K, HOT):
        cluster = lax.broadcasted_iota(jnp.int32, (HOT, TW), 0) + k0
        onehot = jnp.concatenate(
            [(cluster == lab_ref[r:r + 1, :]).astype(F32).astype(BF16) for r in range(TH)], axis=1
        )
        hot_ref[k0:k0 + HOT, :] = onehot
        count_ref[:, k0:k0 + HOT] = dot(ones, onehot, ((1,), (1,)))


def filter_kernel(
    odd_ref, col_near_ref, col_far_ref, wide_ref, hot_ref, count_ref, *refs,
):
    a_ref, b_ref, c_ref, filt_ref, wb_ref, msg_ref = refs[5:]
    odd_col = odd_ref[1] == 1
    near = col_near_ref[0:COL_PIXELS, :].astype(F32).reshape(16, 8, C)
    far = col_far_ref[0:COL_PIXELS, :].astype(F32).reshape(16, 8, C)
    a_ref[:, 8:16, :] = jnp.where(odd_col, near, far)
    a_ref[:, 144:152, :] = jnp.where(odd_col, far, near)
    near = joined(col_near_ref, COL_PIXELS, 8)
    far = joined(col_far_ref, COL_PIXELS, 8)
    sides = unfolded(jnp.where(odd_col, far, near), jnp.where(odd_col, near, far))
    stack = normed_weights(wide_ref, sides)
    centre = stack[:, 0:TW].T
    sides = stack[:, TW:2 * TW].T
    spread_weights(wb_ref, jnp.concatenate([sides[120:128], centre[0:8]], axis=0), 8)
    spread_weights(wb_ref, jnp.concatenate([centre[120:128], sides[0:8]], axis=0), 136)
    sweep(1, (0, 1, 2, 15, 16, 17), wb_ref, a_ref, a_ref, b_ref)
    sweep(2, (0, 1, 2, 3, 14, 15, 16, 17), wb_ref, a_ref, b_ref, c_ref)
    sweep(3, (0, 1, 2, 3, 4, 13, 14, 15, 16, 17), wb_ref, a_ref, c_ref, b_ref)
    sweep(4, (1, 2, 3, 4, 5, 12, 13, 14, 15, 16), wb_ref, a_ref, b_ref, filt_ref)

    high, mid, low = split3(filt_ref[...])
    tall = ((0,), (0,))
    by_high = dot(high, jnp.concatenate([high, mid, low], axis=1), tall)
    by_mid = dot(mid, jnp.concatenate([high, mid], axis=1), tall)
    by_low = dot(low, high, tall)
    gram = by_high[:, 2 * C:] + by_low + by_mid[:, C:]
    gram = gram + (by_high[:, C:2 * C] + by_mid[:, :C])
    gram = gram + by_high[:, :C]

    pieces = jnp.concatenate([high, mid, low], axis=1)
    part = dot(hot_ref[...], pieces, ((1,), (0,)))
    part = (part[:, 2 * C:] + part[:, C:2 * C]) + part[:, :C]
    msg_ref[:, 0:ROWS_OF, :] = part.reshape(PARTS, ROWS_OF, C)
    msg_ref[:, ROWS_OF:ROWS_OF + 4, :] = gram.reshape(PARTS, 4, C)
    for p in range(PARTS):
        lanes = p * ROWS_OF // TW * TW
        msg_ref[p, ROWS_OF + 4:BLOCK, :] = count_ref[0:4, lanes:lanes + TW]


SCALARS = pl.BlockSpec(memory_space=pltpu.SMEM)
VECTORS = pl.BlockSpec(memory_space=pltpu.VMEM)


def pack_rows(odd, x, w):
    shape = jax.ShapeDtypeStruct((ROW_MSG, C), BF16)
    return pl.pallas_call(
        pack_rows_kernel,
        out_shape=(shape, shape),
        in_specs=[SCALARS] + [VECTORS] * 2,
        out_specs=(VECTORS,) * 2,
        compiler_params=pltpu.CompilerParams(vmem_limit_bytes=8 * 2**20),
    )(odd, x.reshape(TH * TW, C), w)


def pack_cols(odd, x, w, near, far):
    shape = jax.ShapeDtypeStruct((COL_MSG, C), BF16)
    return pl.pallas_call(
        pack_cols_kernel,
        out_shape=(
            shape,
            shape,
            jax.ShapeDtypeStruct((4, 24, TW), F32),
            jax.ShapeDtypeStruct((TH * TW, C), BF16),
        ),
        in_specs=[SCALARS] + [VECTORS] * 4,
        out_specs=(VECTORS,) * 4,
        scratch_shapes=[pltpu.VMEM((16, 8, C), F32)] * 2,
        compiler_params=pltpu.CompilerParams(vmem_limit_bytes=8 * 2**20),
    )(odd, x.reshape(TH * TW, C), w, near, far)


FIELD = jax.ShapeDtypeStruct((16, 160, C), F32)
BUFFERS = (
    FIELD,
    FIELD,
    FIELD,
    jax.ShapeDtypeStruct((TH * TW, C), F32),
    jax.ShapeDtypeStruct((4, 16, 160, C), F32),
)


def run_prepare(odd, x, near, far, wide, labels):
    outs = (
        jax.ShapeDtypeStruct((K, TH * TW), BF16),
        jax.ShapeDtypeStruct((8, K), F32),
    ) + BUFFERS
    return pl.pallas_call(
        prepare_kernel,
        out_shape=outs,
        in_specs=[SCALARS] + [VECTORS] * 5,
        out_specs=(VECTORS,) * 7,
        compiler_params=pltpu.CompilerParams(vmem_limit_bytes=16 * 2**20),
        cost_estimate=pl.CostEstimate(flops=2**27, bytes_accessed=2**23, transcendentals=0),
    )(odd, x, near, far, wide, labels)


def run_filter(odd, near, far, wide, hot, counts, *buffers):
    *_, filt, _, msg = pl.pallas_call(
        filter_kernel,
        in_specs=[SCALARS] + [VECTORS] * 10,
        out_shape=BUFFERS + (jax.ShapeDtypeStruct((PARTS, BLOCK, C), F32),),
        out_specs=(VECTORS,) * 6,
        input_output_aliases={6 + q: q for q in range(5)},
        compiler_params=pltpu.CompilerParams(vmem_limit_bytes=16 * 2**20),
    )(odd, near, far, wide, hot, counts, *buffers)
    return filt, msg


def eliminate(g_ref, panel=64, group=8):
    for p0 in range(0, C, panel):
        end = p0 + panel
        for i0 in range(p0, end, group):
            rows = end - i0
            left = g_ref[i0:end, 0:C]
            right = g_ref[i0:end, C:2 * C]
            sub = lax.broadcasted_iota(jnp.int32, (rows, C), 0)
            cols = [jnp.broadcast_to(left[:, i0 + k:i0 + k + 1], (rows, C)) for k in range(group)]
            lrow = [left[k:k + 1, :] for k in range(group)]
            rrow = [right[k:k + 1, :] for k in range(group)]
            a = [[cols[m][k:k + 1, :] for m in range(group)] for k in range(group)]
            for k in range(group):
                root = lax.rsqrt(a[k][k])
                s = [a[k][m] * root for m in range(group)]
                lrow[k] = lrow[k] * root
                rrow[k] = rrow[k] * root
                cols[k] = cols[k] * root
                for m in range(k + 1, group):
                    for n in range(m, group):
                        a[m][n] = a[m][n] - s[m] * s[n]
                    lrow[m] = lrow[m] - s[m] * lrow[k]
                    rrow[m] = rrow[m] - s[m] * rrow[k]
                    cols[m] = cols[m] - s[m] * cols[k]
            if rows > group:
                for k in range(group):
                    factor = jnp.where(sub >= group, cols[k], 0.0)
                    left = left - factor * lrow[k]
                    right = right - factor * rrow[k]
            for k in range(group):
                left = jnp.where(sub == k, lrow[k], left)
                right = jnp.where(sub == k, rrow[k], right)
            g_ref[i0:end, 0:C] = left
            g_ref[i0:end, C:2 * C] = right
        if end < C:
            uh, um, ul = split3(g_ref[p0:end, 0:C])
            fh, fm, fl = split3(g_ref[p0:end, :])
            lhs = jnp.concatenate([uh, um, ul, um, uh, uh], axis=0)
            rhs = jnp.concatenate([fl, fm, fh, fh, fm, fh], axis=0)
            update = dot(lhs, rhs, ((0,), (0,)))
            g_ref[end:C, :] = g_ref[end:C, :] - update[end:C, :]


def finish_kernel(msg_ref, filt_ref, best_ref, cent_ref, g_ref, c_ref, sem, *, total):
    for p in range(PARTS):
        g_ref[4 * p:4 * p + 4, 0:C] = msg_ref[p, ROWS_OF:ROWS_OF + 4, :]
    row = lax.broadcasted_iota(jnp.int32, (C, C), 0)
    col = lax.broadcasted_iota(jnp.int32, (C, C), 1)
    g_ref[:, C:2 * C] = jnp.where(row == col, 1.0, 0.0).astype(F32)

    eliminate(g_ref)
    inverse = g_ref[:, C:2 * C] * math.sqrt(total)
    ih, im, il = split3(inverse)
    lhs = jnp.concatenate([il, im, ih, im, ih, ih], axis=1)

    def times_inverse(x, transposed):
        xh, xm, xl = split3(x)
        rhs = jnp.concatenate([xh, xm, xl, xh, xm, xh], axis=1)
        if transposed:
            return dot(lhs, rhs, ((1,), (1,)))
        return dot(rhs, lhs, ((1,), (1,)))

    sums = msg_ref[:, 0:ROWS_OF, :].reshape(K, C)
    counts = jnp.concatenate(
        [jnp.broadcast_to(msg_ref[p, ROWS_OF + 4:ROWS_OF + 5, :], (C, C)).T for p in range(0, PARTS, 4)],
        axis=0,
    )
    c_ref[...] = times_inverse(sums, False) / (counts + 1.0)
    copy = pltpu.make_async_copy(c_ref, cent_ref, sem)
    copy.start()
    whitened_t = times_inverse(filt_ref[...], True)
    norms = jnp.sum(whitened_t * whitened_t, axis=0, keepdims=True)
    wh, wm, wl = split3(whitened_t)
    w_all = jnp.concatenate([wl, wm, wh, wm, wh, wh], axis=0)
    cent = c_ref[...]
    cent_norm = jnp.sum(cent * cent, axis=1, keepdims=True)
    ch, cm, cl = split3(-2.0 * cent)
    c_all = jnp.concatenate([ch, cm, cl, ch, cm, ch], axis=1)
    value = dot(c_all, w_all, ((1,), (0,))) + cent_norm
    best = jnp.min(value, axis=0, keepdims=True)
    result = (norms + best) / C
    for r in range(TH):
        best_ref[r:r + 1, :] = result[:, r * TW:(r + 1) * TW]
    copy.wait()


def run_finish(msg, filt, total):

    return pl.pallas_call(
        functools.partial(finish_kernel, total=total),
        out_shape=(
            jax.ShapeDtypeStruct((TH, TW), F32),
            jax.ShapeDtypeStruct((K, C), F32),
        ),
        out_specs=(VECTORS, pl.BlockSpec(memory_space=pltpu.HBM)),
        scratch_shapes=[pltpu.VMEM((C, 2 * C), F32), pltpu.VMEM((K, C), F32), pltpu.SemaphoreType.DMA],
        compiler_params=pltpu.CompilerParams(vmem_limit_bytes=32 * 2**20),
    )(msg, filt)


GY = ("xh", "y", "c")
GX = ("zh", "zl", "xl")


def swap(near, far, axes, size):
    near_pairs = [(i, i ^ 1) for i in range(size)]
    far_pairs = [(i, i + 1) for i in range(1, size - 1, 2)]
    far_pairs = far_pairs + [(b, a) for a, b in far_pairs]
    far = lax.ppermute(far, axes, far_pairs)
    return lax.ppermute(near, axes, near_pairs), far


def exchange(x, axes):
    return lax.all_to_all(x, axes, 0, 0)


def spread(x, axes, count):
    return exchange(jnp.broadcast_to(x[None], (count,) + x.shape), axes)


def reduce_all(msg):
    piece = jnp.sum(exchange(msg, ("c", "xh", "y", "xl")), axis=0)
    piece = jnp.sum(spread(piece, "zl", 4), axis=0)
    piece = jnp.sum(spread(piece, "zh", 4), axis=0)
    half = spread(piece, ("xh", "y", "xl"), PARTS // 2)
    return lax.all_gather(half, "c", axis=0, tiled=True)


def on_device(embeddings, affinity, assignment):
    n_gy, n_gx = 16, 32
    odd = jnp.stack([lax.axis_index("c"), lax.axis_index("xl")]).astype(jnp.int32)
    rows = swap(*pack_rows(odd, embeddings, affinity), GY, n_gy)
    near, far, wide, pixels = pack_cols(odd, embeddings, affinity, *rows)
    prepared = run_prepare(odd, pixels, *rows, wide, assignment)
    cols = swap(near, far, GX, n_gx)
    filt, msg = run_filter(odd, *cols, wide, *prepared)
    msg = reduce_all(msg)
    return run_finish(msg, filt, TH * TW * n_gy * n_gx)


def solution(mesh):
    inner = Mesh(mesh.devices.reshape(2, 4, 2, 4, 4, 2), GY + GX)
    return jax.shard_map(
        on_device,
        mesh=inner,
        in_specs=(P(GY, GX, None), P(None, GY, GX), P(GY, GX)),
        out_specs=(P(GY, GX), P()),
        check_vma=False,
    )
```

```python
import functools
import math

import jax
import jax.numpy as jnp
from jax import lax
from jax.experimental import pallas as pl
from jax.experimental.pallas import tpu as pltpu
from jax.sharding import Mesh
from jax.sharding import PartitionSpec as P

K = 1024
C = 128
TH = 8
TW = 128
HALO = 4
DEGREE = 4
COEFFS = (0.5, 0.45, 0.35, 0.25, 0.15)
POWERS = (
    COEFFS[0] - COEFFS[2] + COEFFS[4],
    COEFFS[1] - 3.0 * COEFFS[3],
    2.0 * COEFFS[2] - 8.0 * COEFFS[4],
    4.0 * COEFFS[3],
    8.0 * COEFFS[4],
)
PARTS = 32
HOT = 256
BLOCK = 40
ROWS_OF = K // PARTS
F32 = jnp.float32
BF16 = jnp.bfloat16


def split3(x):
    high = x.astype(BF16)
    rest = x - high.astype(F32)
    mid = rest.astype(BF16)
    low = (rest - mid.astype(F32)).astype(BF16)
    return high, mid, low


def dot(a, b, dims):
    return lax.dot_general(a, b, (dims, ((), ())), preferred_element_type=F32)


ROW_PIXELS = HALO * TW
ROW_MSG = ROW_PIXELS + 3 * 32
COL_PIXELS = 16 * 8
COL_MSG = COL_PIXELS + 3 * 8


def joined(ref, first, count):
    pieces = ref[first:first + 3 * count, :].astype(F32)
    return (pieces[0:count] + pieces[count:2 * count]) + pieces[2 * count:]


def folded(x, first):
    lane = lax.broadcasted_iota(jnp.int32, (8, TW), 1) // 8
    out = jnp.zeros((8, TW), F32)
    for v in range(12):
        moved = pltpu.roll(x[8 * v:8 * v + 8], (8 * v - first) % TW, 1)
        out = jnp.where(lane == v, moved, out)
    return out


def unfolded(low, high):
    lane = lax.broadcasted_iota(jnp.int32, (8, TW), 1)
    return jnp.concatenate(
        [
            jnp.where(
                lane < 64,
                pltpu.roll(low, -8 * v % TW, 1),
                pltpu.roll(high, (TW - 8 - 8 * v) % TW, 1),
            )
            for v in range(12)
        ],
        axis=0,
    )


def pack_rows_kernel(odd_ref, x_ref, w_ref, near_ref, far_ref):
    planes = jnp.concatenate(split3(w_ref[...].reshape(32, TW)), axis=0)
    odd = odd_ref[0]
    for ref, first in ((near_ref, 1 - odd), (far_ref, odd)):
        pixels = pl.ds(pl.multiple_of(first * ROW_PIXELS, ROW_PIXELS), ROW_PIXELS)
        ref[0:ROW_PIXELS, :] = x_ref[pixels, :]
        ref[ROW_PIXELS:ROW_MSG, :] = planes


def pack_cols_kernel(
    odd_ref, x_ref, w_ref, row_near_ref, row_far_ref,
    near_ref, far_ref, wide_ref, x_out_ref, lo_ref, hi_ref,
):
    x_out_ref[...] = x_ref[...]
    odd_row = odd_ref[0] == 1
    near_at = jnp.where(odd_row, 0, 1)
    for ref, at in ((row_near_ref, near_at), (row_far_ref, 1 - near_at)):
        weights = joined(ref, ROW_PIXELS, 32)
        for d in range(4):
            wide_ref[d, pl.ds(pl.multiple_of(16 * at, 8), 8), :] = weights[8 * d:8 * d + 8]
        for r in range(HALO):
            lo_ref[12 * at + r] = ref[r * TW:r * TW + 16, :].astype(F32)[0:8]
            hi_ref[12 * at + r] = ref[r * TW + TW - 16:r * TW + TW, :].astype(F32)[8:16]
    for d in range(4):
        wide_ref[d, 8:16, :] = w_ref[d]
    for r in range(TH):
        lo_ref[HALO + r] = x_ref[r * TW:r * TW + 16, :].astype(F32)[0:8]
        hi_ref[HALO + r] = x_ref[r * TW + TW - 16:r * TW + TW, :].astype(F32)[8:16]
    odd_col = odd_ref[1] == 1
    wide = wide_ref[...].reshape(96, TW)
    low, high = folded(wide, 0), folded(wide, TW - 8)
    for ref, part in (
        (near_ref, jnp.where(odd_col, low, high)), (far_ref, jnp.where(odd_col, high, low))
    ):
        ref[COL_PIXELS:COL_MSG, :] = jnp.concatenate([q.astype(F32) for q in split3(part)], axis=0).astype(BF16)
    low = lo_ref[...].reshape(COL_PIXELS, C)
    high = hi_ref[...].reshape(COL_PIXELS, C)
    near_ref[0:COL_PIXELS, :] = jnp.where(odd_col, low, high).astype(BF16)
    far_ref[0:COL_PIXELS, :] = jnp.where(odd_col, high, low).astype(BF16)


def normed_weights(wide_ref, sides):
    def weights(d):
        return jnp.concatenate([wide_ref[d], sides[24 * d:24 * d + 24]], axis=1)

    def right(x):
        return pltpu.roll(x, 255, 1)

    def left(x):
        return pltpu.roll(x, 1, 1)

    def down(x):
        return pltpu.roll(x, 23, 0)

    def up(x):
        return pltpu.roll(x, 1, 0)

    east, south, diag, anti = weights(0), weights(1), weights(2), weights(3)
    degree = east + left(east)
    degree = degree + south + up(south)
    degree = degree + diag + up(left(diag))
    degree = degree + anti + up(right(anti))
    scale = jnp.where(degree > 0.0, lax.rsqrt(jnp.where(degree > 0.0, degree, 1.0)), 0.0)
    below = down(scale)
    normed = (
        scale * east * right(scale),
        scale * south * below,
        scale * diag * right(below),
        scale * anti * left(below),
    )
    return jnp.concatenate(normed + (jnp.zeros((32, 256), F32),), axis=0)


def spread_weights(wb_ref, columns, first):
    count = columns.shape[0]
    for d in range(4):
        for r in range(16):
            k = d * 24 + r + 4
            wb_ref[d, r, first:first + count, :] = jnp.broadcast_to(columns[:, k:k + 1], (count, C))


def apply_rows(wb_ref, src, r, rows, s):
    x, w = {}, {}

    def field(q, off):
        if (q, off) not in x:
            x[q, off] = src[r + q, s + off:s + off + 8, :]
        return x[q, off]

    def weight(d, q, off):
        if (d, q, off) not in w:
            w[d, q, off] = wb_ref[d, r + q, s + off:s + off + 8, :]
        return w[d, q, off]

    outs = []
    for q in range(rows):
        out = weight(0, q, 0) * field(q, 1) + weight(0, q, -1) * field(q, -1)
        out = out + weight(1, q - 1, 0) * field(q - 1, 0)
        out = out + weight(2, q - 1, -1) * field(q - 1, -1)
        out = out + weight(3, q - 1, 1) * field(q - 1, 1)
        out = out + weight(1, q, 0) * field(q + 1, 0)
        out = out + weight(2, q, 0) * field(q + 1, 1)
        outs.append(out + weight(3, q, 0) * field(q + 1, -1))
    return outs


def sweep(step, tiles, wb_ref, start_ref, src, dst):
    rows = (16 - 2 * step) // 2
    for r in (step, step + rows):
        for t in tiles:
            s = 8 + 8 * t
            for q, new in enumerate(apply_rows(wb_ref, src, r, rows, s)):
                start = start_ref[r + q, s:s + 8, :]
                if step == 1:
                    new = POWERS[4] * new + POWERS[3] * start
                else:
                    new = new + POWERS[DEGREE - step] * start
                if step < DEGREE:
                    dst[r + q, s:s + 8, :] = new
                else:
                    pixel = (r + q - 4) * TW + s - 16
                    dst[pixel:pixel + 8, :] = new


def prepare_kernel(
    odd_ref, x_ref, row_near_ref, row_far_ref, wide_ref, lab_ref,
    hot_ref, count_ref, a_ref, b_ref, c_ref, filt_ref, wb_ref,
):
    zeros8 = jnp.zeros((16, 8, C), F32)
    for buf in (a_ref, b_ref, c_ref, wb_ref.at[0], wb_ref.at[1], wb_ref.at[2], wb_ref.at[3]):
        buf[:, 0:8, :] = zeros8
        buf[:, 152:160, :] = zeros8
    near_at = jnp.where(odd_ref[0] == 1, 0, 1)
    for ref, at in ((row_near_ref, near_at), (row_far_ref, 1 - near_at)):
        a_ref[pl.ds(12 * at, HALO), 16:144, :] = ref[0:ROW_PIXELS, :].astype(F32).reshape(HALO, TW, C)
    a_ref[4:12, 16:144, :] = x_ref[...].astype(F32).reshape(TH, TW, C)
    stack = normed_weights(wide_ref, jnp.zeros((96, TW), F32))
    spread_weights(wb_ref, stack[:, 0:TW].T[8:120], 24)
    sweep(1, range(3, 15), wb_ref, a_ref, a_ref, b_ref)
    sweep(2, range(4, 14), wb_ref, a_ref, b_ref, c_ref)
    sweep(3, range(5, 13), wb_ref, a_ref, c_ref, b_ref)
    sweep(4, range(6, 12), wb_ref, a_ref, b_ref, filt_ref)
    ones = jnp.ones((8, TH * TW), BF16)
    for k0 in range(0, K, HOT):
        cluster = lax.broadcasted_iota(jnp.int32, (HOT, TW), 0) + k0
        onehot = jnp.concatenate(
            [(cluster == lab_ref[r:r + 1, :]).astype(F32).astype(BF16) for r in range(TH)], axis=1
        )
        hot_ref[k0:k0 + HOT, :] = onehot
        count_ref[:, k0:k0 + HOT] = dot(ones, onehot, ((1,), (1,)))


def filter_kernel(
    odd_ref, col_near_ref, col_far_ref, wide_ref, hot_ref, count_ref, *refs,
):
    a_ref, b_ref, c_ref, filt_ref, wb_ref, msg_ref = refs[5:]
    odd_col = odd_ref[1] == 1
    near = col_near_ref[0:COL_PIXELS, :].astype(F32).reshape(16, 8, C)
    far = col_far_ref[0:COL_PIXELS, :].astype(F32).reshape(16, 8, C)
    a_ref[:, 8:16, :] = jnp.where(odd_col, near, far)
    a_ref[:, 144:152, :] = jnp.where(odd_col, far, near)
    near = joined(col_near_ref, COL_PIXELS, 8)
    far = joined(col_far_ref, COL_PIXELS, 8)
    sides = unfolded(jnp.where(odd_col, far, near), jnp.where(odd_col, near, far))
    stack = normed_weights(wide_ref, sides)
    centre = stack[:, 0:TW].T
    sides = stack[:, TW:2 * TW].T
    spread_weights(wb_ref, jnp.concatenate([sides[120:128], centre[0:8]], axis=0), 8)
    spread_weights(wb_ref, jnp.concatenate([centre[120:128], sides[0:8]], axis=0), 136)
    sweep(1, (0, 1, 2, 15, 16, 17), wb_ref, a_ref, a_ref, b_ref)
    sweep(2, (0, 1, 2, 3, 14, 15, 16, 17), wb_ref, a_ref, b_ref, c_ref)
    sweep(3, (0, 1, 2, 3, 4, 13, 14, 15, 16, 17), wb_ref, a_ref, c_ref, b_ref)
    sweep(4, (1, 2, 3, 4, 5, 12, 13, 14, 15, 16), wb_ref, a_ref, b_ref, filt_ref)

    high, mid, low = split3(filt_ref[...])
    tall = ((0,), (0,))
    by_high = dot(high, jnp.concatenate([high, mid, low], axis=1), tall)
    by_mid = dot(mid, jnp.concatenate([high, mid], axis=1), tall)
    by_low = dot(low, high, tall)
    gram = by_high[:, 2 * C:] + by_low + by_mid[:, C:]
    gram = gram + (by_high[:, C:2 * C] + by_mid[:, :C])
    gram = gram + by_high[:, :C]

    pieces = jnp.concatenate([high, mid], axis=1)
    part = dot(hot_ref[...], pieces, ((1,), (0,)))
    part = part[:, C:] + part[:, :C]
    msg_ref[:, 0:ROWS_OF, :] = part.reshape(PARTS, ROWS_OF, C)
    msg_ref[:, ROWS_OF:ROWS_OF + 4, :] = gram.reshape(PARTS, 4, C)
    for p in range(PARTS):
        lanes = p * ROWS_OF // TW * TW
        msg_ref[p, ROWS_OF + 4:BLOCK, :] = count_ref[0:4, lanes:lanes + TW]


SCALARS = pl.BlockSpec(memory_space=pltpu.SMEM)
VECTORS = pl.BlockSpec(memory_space=pltpu.VMEM)


def pack_rows(odd, x, w):
    shape = jax.ShapeDtypeStruct((ROW_MSG, C), BF16)
    return pl.pallas_call(
        pack_rows_kernel,
        out_shape=(shape, shape),
        in_specs=[SCALARS] + [VECTORS] * 2,
        out_specs=(VECTORS,) * 2,
        compiler_params=pltpu.CompilerParams(vmem_limit_bytes=8 * 2**20),
    )(odd, x.reshape(TH * TW, C), w)


def pack_cols(odd, x, w, near, far):
    shape = jax.ShapeDtypeStruct((COL_MSG, C), BF16)
    return pl.pallas_call(
        pack_cols_kernel,
        out_shape=(
            shape,
            shape,
            jax.ShapeDtypeStruct((4, 24, TW), F32),
            jax.ShapeDtypeStruct((TH * TW, C), BF16),
        ),
        in_specs=[SCALARS] + [VECTORS] * 4,
        out_specs=(VECTORS,) * 4,
        scratch_shapes=[pltpu.VMEM((16, 8, C), F32)] * 2,
        compiler_params=pltpu.CompilerParams(vmem_limit_bytes=8 * 2**20),
    )(odd, x.reshape(TH * TW, C), w, near, far)


FIELD = jax.ShapeDtypeStruct((16, 160, C), F32)
BUFFERS = (
    FIELD,
    FIELD,
    FIELD,
    jax.ShapeDtypeStruct((TH * TW, C), F32),
    jax.ShapeDtypeStruct((4, 16, 160, C), F32),
)


def run_prepare(odd, x, near, far, wide, labels):
    outs = (
        jax.ShapeDtypeStruct((K, TH * TW), BF16),
        jax.ShapeDtypeStruct((8, K), F32),
    ) + BUFFERS
    return pl.pallas_call(
        prepare_kernel,
        out_shape=outs,
        in_specs=[SCALARS] + [VECTORS] * 5,
        out_specs=(VECTORS,) * 7,
        compiler_params=pltpu.CompilerParams(vmem_limit_bytes=16 * 2**20),
        cost_estimate=pl.CostEstimate(flops=2**27, bytes_accessed=2**23, transcendentals=0),
    )(odd, x, near, far, wide, labels)


def run_filter(odd, near, far, wide, hot, counts, *buffers):
    *_, filt, _, msg = pl.pallas_call(
        filter_kernel,
        in_specs=[SCALARS] + [VECTORS] * 10,
        out_shape=BUFFERS + (jax.ShapeDtypeStruct((PARTS, BLOCK, C), F32),),
        out_specs=(VECTORS,) * 6,
        input_output_aliases={6 + q: q for q in range(5)},
        compiler_params=pltpu.CompilerParams(vmem_limit_bytes=16 * 2**20),
    )(odd, near, far, wide, hot, counts, *buffers)
    return filt, msg


def eliminate(g_ref, panel=64, group=8):
    for p0 in range(0, C, panel):
        end = p0 + panel
        for i0 in range(p0, end, group):
            rows = end - i0
            left = g_ref[i0:end, 0:C]
            right = g_ref[i0:end, C:2 * C]
            sub = lax.broadcasted_iota(jnp.int32, (rows, C), 0)
            cols = [jnp.broadcast_to(left[:, i0 + k:i0 + k + 1], (rows, C)) for k in range(group)]
            lrow = [left[k:k + 1, :] for k in range(group)]
            rrow = [right[k:k + 1, :] for k in range(group)]
            a = [[cols[m][k:k + 1, :] for m in range(group)] for k in range(group)]
            for k in range(group):
                root = lax.rsqrt(a[k][k])
                s = [a[k][m] * root for m in range(group)]
                lrow[k] = lrow[k] * root
                rrow[k] = rrow[k] * root
                cols[k] = cols[k] * root
                for m in range(k + 1, group):
                    for n in range(m, group):
                        a[m][n] = a[m][n] - s[m] * s[n]
                    lrow[m] = lrow[m] - s[m] * lrow[k]
                    rrow[m] = rrow[m] - s[m] * rrow[k]
                    cols[m] = cols[m] - s[m] * cols[k]
            if rows > group:
                for k in range(group):
                    factor = jnp.where(sub >= group, cols[k], 0.0)
                    left = left - factor * lrow[k]
                    right = right - factor * rrow[k]
            for k in range(group):
                left = jnp.where(sub == k, lrow[k], left)
                right = jnp.where(sub == k, rrow[k], right)
            g_ref[i0:end, 0:C] = left
            g_ref[i0:end, C:2 * C] = right
        if end < C:
            uh, um, ul = split3(g_ref[p0:end, 0:C])
            fh, fm, fl = split3(g_ref[p0:end, :])
            lhs = jnp.concatenate([uh, um, ul, um, uh, uh], axis=0)
            rhs = jnp.concatenate([fl, fm, fh, fh, fm, fh], axis=0)
            update = dot(lhs, rhs, ((0,), (0,)))
            g_ref[end:C, :] = g_ref[end:C, :] - update[end:C, :]


def finish_kernel(msg_ref, filt_ref, best_ref, cent_ref, g_ref, c_ref, sem, *, total):
    for p in range(PARTS):
        g_ref[4 * p:4 * p + 4, 0:C] = msg_ref[p, ROWS_OF:ROWS_OF + 4, :]
    row = lax.broadcasted_iota(jnp.int32, (C, C), 0)
    col = lax.broadcasted_iota(jnp.int32, (C, C), 1)
    g_ref[:, C:2 * C] = jnp.where(row == col, 1.0, 0.0).astype(F32)

    eliminate(g_ref)
    inverse = g_ref[:, C:2 * C] * math.sqrt(total)
    ih, im, il = split3(inverse)
    lhs = jnp.concatenate([il, im, ih, im, ih, ih], axis=1)

    def times_inverse(x, transposed):
        xh, xm, xl = split3(x)
        rhs = jnp.concatenate([xh, xm, xl, xh, xm, xh], axis=1)
        if transposed:
            return dot(lhs, rhs, ((1,), (1,)))
        return dot(rhs, lhs, ((1,), (1,)))

    sums = msg_ref[:, 0:ROWS_OF, :].reshape(K, C)
    counts = jnp.concatenate(
        [jnp.broadcast_to(msg_ref[p, ROWS_OF + 4:ROWS_OF + 5, :], (C, C)).T for p in range(0, PARTS, 4)],
        axis=0,
    )
    c_ref[...] = times_inverse(sums, False) / (counts + 1.0)
    copy = pltpu.make_async_copy(c_ref, cent_ref, sem)
    copy.start()
    whitened_t = times_inverse(filt_ref[...], True)
    norms = jnp.sum(whitened_t * whitened_t, axis=0, keepdims=True)
    wh, wm, _ = split3(whitened_t)
    w_all = jnp.concatenate([wm, wh, wh], axis=0)
    cent = c_ref[...]
    cent_norm = jnp.sum(cent * cent, axis=1, keepdims=True)
    ch, cm, _ = split3(-2.0 * cent)
    c_all = jnp.concatenate([ch, cm, ch], axis=1)
    value = dot(c_all, w_all, ((1,), (0,))) + cent_norm
    best = jnp.min(value, axis=0, keepdims=True)
    result = (norms + best) / C
    for r in range(TH):
        best_ref[r:r + 1, :] = result[:, r * TW:(r + 1) * TW]
    copy.wait()


def run_finish(msg, filt, total):

    return pl.pallas_call(
        functools.partial(finish_kernel, total=total),
        out_shape=(
            jax.ShapeDtypeStruct((TH, TW), F32),
            jax.ShapeDtypeStruct((K, C), F32),
        ),
        out_specs=(VECTORS, pl.BlockSpec(memory_space=pltpu.HBM)),
        scratch_shapes=[pltpu.VMEM((C, 2 * C), F32), pltpu.VMEM((K, C), F32), pltpu.SemaphoreType.DMA],
        compiler_params=pltpu.CompilerParams(vmem_limit_bytes=32 * 2**20),
    )(msg, filt)


GY = ("xh", "y", "c")
GX = ("zh", "zl", "xl")


def swap(near, far, axes, size):
    near_pairs = [(i, i ^ 1) for i in range(size)]
    far_pairs = [(i, i + 1) for i in range(1, size - 1, 2)]
    far_pairs = far_pairs + [(b, a) for a, b in far_pairs]
    far = lax.ppermute(far, axes, far_pairs)
    return lax.ppermute(near, axes, near_pairs), far


def exchange(x, axes):
    return lax.all_to_all(x, axes, 0, 0)


def spread(x, axes, count):
    return exchange(jnp.broadcast_to(x[None], (count,) + x.shape), axes)


def reduce_all(msg):
    piece = jnp.sum(exchange(msg, ("c", "xh", "y", "xl")), axis=0)
    piece = jnp.sum(spread(piece, "zl", 4), axis=0)
    piece = jnp.sum(spread(piece, "zh", 4), axis=0)
    half = spread(piece, ("xh", "y", "xl"), PARTS // 2)
    return lax.all_gather(half, "c", axis=0, tiled=True)


def on_device(embeddings, affinity, assignment):
    n_gy, n_gx = 16, 32
    odd = jnp.stack([lax.axis_index("c"), lax.axis_index("xl")]).astype(jnp.int32)
    rows = swap(*pack_rows(odd, embeddings, affinity), GY, n_gy)
    near, far, wide, pixels = pack_cols(odd, embeddings, affinity, *rows)
    prepared = run_prepare(odd, pixels, *rows, wide, assignment)
    cols = swap(near, far, GX, n_gx)
    filt, msg = run_filter(odd, *cols, wide, *prepared)
    msg = reduce_all(msg)
    return run_finish(msg, filt, TH * TW * n_gy * n_gx)


def solution(mesh):
    inner = Mesh(mesh.devices.reshape(2, 4, 2, 4, 4, 2), GY + GX)
    return jax.shard_map(
        on_device,
        mesh=inner,
        in_specs=(P(GY, GX, None), P(None, GY, GX), P(GY, GX)),
        out_specs=(P(GY, GX), P()),
        check_vma=False,
    )
```

```python
import functools
import math

import jax
import jax.numpy as jnp
from jax import lax
from jax.experimental import pallas as pl
from jax.experimental.pallas import tpu as pltpu
from jax.sharding import Mesh
from jax.sharding import PartitionSpec as P

K = 1024
C = 128
TH = 8
TW = 128
HALO = 4
DEGREE = 4
COEFFS = (0.5, 0.45, 0.35, 0.25, 0.15)
POWERS = (
    COEFFS[0] - COEFFS[2] + COEFFS[4],
    COEFFS[1] - 3.0 * COEFFS[3],
    2.0 * COEFFS[2] - 8.0 * COEFFS[4],
    4.0 * COEFFS[3],
    8.0 * COEFFS[4],
)
PARTS = 32
HOT = 256
BLOCK = 40
ROWS_OF = K // PARTS
F32 = jnp.float32
BF16 = jnp.bfloat16


def split3(x):
    high = x.astype(BF16)
    rest = x - high.astype(F32)
    mid = rest.astype(BF16)
    low = (rest - mid.astype(F32)).astype(BF16)
    return high, mid, low


def dot(a, b, dims):
    return lax.dot_general(a, b, (dims, ((), ())), preferred_element_type=F32)


ROW_PIXELS = HALO * TW
ROW_MSG = ROW_PIXELS + 3 * 32
COL_PIXELS = 16 * 8
COL_MSG = COL_PIXELS + 3 * 8


def joined(ref, first, count):
    pieces = ref[first:first + 3 * count, :].astype(F32)
    return (pieces[0:count] + pieces[count:2 * count]) + pieces[2 * count:]


def folded(x, first):
    lane = lax.broadcasted_iota(jnp.int32, (8, TW), 1) // 8
    out = jnp.zeros((8, TW), F32)
    for v in range(12):
        moved = pltpu.roll(x[8 * v:8 * v + 8], (8 * v - first) % TW, 1)
        out = jnp.where(lane == v, moved, out)
    return out


def unfolded(low, high):
    lane = lax.broadcasted_iota(jnp.int32, (8, TW), 1)
    return jnp.concatenate(
        [
            jnp.where(
                lane < 64,
                pltpu.roll(low, -8 * v % TW, 1),
                pltpu.roll(high, (TW - 8 - 8 * v) % TW, 1),
            )
            for v in range(12)
        ],
        axis=0,
    )


def pack_rows_kernel(odd_ref, x_ref, w_ref, near_ref, far_ref):
    planes = jnp.concatenate(split3(w_ref[...].reshape(32, TW)), axis=0)
    odd = odd_ref[0]
    for ref, first in ((near_ref, 1 - odd), (far_ref, odd)):
        pixels = pl.ds(pl.multiple_of(first * ROW_PIXELS, ROW_PIXELS), ROW_PIXELS)
        ref[0:ROW_PIXELS, :] = x_ref[pixels, :]
        ref[ROW_PIXELS:ROW_MSG, :] = planes


def pack_cols_kernel(
    odd_ref, x_ref, w_ref, row_near_ref, row_far_ref,
    near_ref, far_ref, wide_ref, x_out_ref, lo_ref, hi_ref,
):
    x_out_ref[...] = x_ref[...]
    odd_row = odd_ref[0] == 1
    near_at = jnp.where(odd_row, 0, 1)
    for ref, at in ((row_near_ref, near_at), (row_far_ref, 1 - near_at)):
        weights = joined(ref, ROW_PIXELS, 32)
        for d in range(4):
            wide_ref[d, pl.ds(pl.multiple_of(16 * at, 8), 8), :] = weights[8 * d:8 * d + 8]
        for r in range(HALO):
            lo_ref[12 * at + r] = ref[r * TW:r * TW + 16, :].astype(F32)[0:8]
            hi_ref[12 * at + r] = ref[r * TW + TW - 16:r * TW + TW, :].astype(F32)[8:16]
    for d in range(4):
        wide_ref[d, 8:16, :] = w_ref[d]
    for r in range(TH):
        lo_ref[HALO + r] = x_ref[r * TW:r * TW + 16, :].astype(F32)[0:8]
        hi_ref[HALO + r] = x_ref[r * TW + TW - 16:r * TW + TW, :].astype(F32)[8:16]
    odd_col = odd_ref[1] == 1
    wide = wide_ref[...].reshape(96, TW)
    low, high = folded(wide, 0), folded(wide, TW - 8)
    for ref, part in (
        (near_ref, jnp.where(odd_col, low, high)), (far_ref, jnp.where(odd_col, high, low))
    ):
        ref[COL_PIXELS:COL_MSG, :] = jnp.concatenate([q.astype(F32) for q in split3(part)], axis=0).astype(BF16)
    low = lo_ref[...].reshape(COL_PIXELS, C)
    high = hi_ref[...].reshape(COL_PIXELS, C)
    near_ref[0:COL_PIXELS, :] = jnp.where(odd_col, low, high).astype(BF16)
    far_ref[0:COL_PIXELS, :] = jnp.where(odd_col, high, low).astype(BF16)


def normed_weights(wide_ref, sides):
    def weights(d):
        return jnp.concatenate([wide_ref[d], sides[24 * d:24 * d + 24]], axis=1)

    def right(x):
        return pltpu.roll(x, 255, 1)

    def left(x):
        return pltpu.roll(x, 1, 1)

    def down(x):
        return pltpu.roll(x, 23, 0)

    def up(x):
        return pltpu.roll(x, 1, 0)

    east, south, diag, anti = weights(0), weights(1), weights(2), weights(3)
    degree = east + left(east)
    degree = degree + south + up(south)
    degree = degree + diag + up(left(diag))
    degree = degree + anti + up(right(anti))
    scale = jnp.where(degree > 0.0, lax.rsqrt(jnp.where(degree > 0.0, degree, 1.0)), 0.0)
    below = down(scale)
    normed = (
        scale * east * right(scale),
        scale * south * below,
        scale * diag * right(below),
        scale * anti * left(below),
    )
    return jnp.concatenate(normed + (jnp.zeros((32, 256), F32),), axis=0)


def spread_weights(wb_ref, columns, first):
    count = columns.shape[0]
    for d in range(4):
        for r in range(16):
            k = d * 24 + r + 4
            wb_ref[d, r, first:first + count, :] = jnp.broadcast_to(columns[:, k:k + 1], (count, C))


def apply_rows(wb_ref, src, r, rows, s):
    x, w = {}, {}

    def field(q, off):
        if (q, off) not in x:
            x[q, off] = src[r + q, s + off:s + off + 8, :]
        return x[q, off]

    def weight(d, q, off):
        if (d, q, off) not in w:
            w[d, q, off] = wb_ref[d, r + q, s + off:s + off + 8, :]
        return w[d, q, off]

    outs = []
    for q in range(rows):
        out = weight(0, q, 0) * field(q, 1) + weight(0, q, -1) * field(q, -1)
        out = out + weight(1, q - 1, 0) * field(q - 1, 0)
        out = out + weight(2, q - 1, -1) * field(q - 1, -1)
        out = out + weight(3, q - 1, 1) * field(q - 1, 1)
        out = out + weight(1, q, 0) * field(q + 1, 0)
        out = out + weight(2, q, 0) * field(q + 1, 1)
        outs.append(out + weight(3, q, 0) * field(q + 1, -1))
    return outs


def sweep(step, tiles, wb_ref, start_ref, src, dst):
    rows = (16 - 2 * step) // 2
    for r in (step, step + rows):
        for t in tiles:
            s = 8 + 8 * t
            for q, new in enumerate(apply_rows(wb_ref, src, r, rows, s)):
                start = start_ref[r + q, s:s + 8, :]
                if step == 1:
                    new = POWERS[4] * new + POWERS[3] * start
                else:
                    new = new + POWERS[DEGREE - step] * start
                if step < DEGREE:
                    dst[r + q, s:s + 8, :] = new
                else:
                    pixel = (r + q - 4) * TW + s - 16
                    dst[pixel:pixel + 8, :] = new


def prepare_kernel(
    odd_ref, x_ref, row_near_ref, row_far_ref, wide_ref, lab_ref,
    hot_ref, count_ref, a_ref, b_ref, c_ref, filt_ref, wb_ref,
):
    zeros8 = jnp.zeros((16, 8, C), F32)
    for buf in (a_ref, b_ref, c_ref, wb_ref.at[0], wb_ref.at[1], wb_ref.at[2], wb_ref.at[3]):
        buf[:, 0:8, :] = zeros8
        buf[:, 152:160, :] = zeros8
    near_at = jnp.where(odd_ref[0] == 1, 0, 1)
    for ref, at in ((row_near_ref, near_at), (row_far_ref, 1 - near_at)):
        a_ref[pl.ds(12 * at, HALO), 16:144, :] = ref[0:ROW_PIXELS, :].astype(F32).reshape(HALO, TW, C)
    a_ref[4:12, 16:144, :] = x_ref[...].astype(F32).reshape(TH, TW, C)
    stack = normed_weights(wide_ref, jnp.zeros((96, TW), F32))
    spread_weights(wb_ref, stack[:, 0:TW].T[8:120], 24)
    sweep(1, range(3, 15), wb_ref, a_ref, a_ref, b_ref)
    sweep(2, range(4, 14), wb_ref, a_ref, b_ref, c_ref)
    sweep(3, range(5, 13), wb_ref, a_ref, c_ref, b_ref)
    sweep(4, range(6, 12), wb_ref, a_ref, b_ref, filt_ref)
    ones = jnp.ones((8, TH * TW), BF16)
    for k0 in range(0, K, HOT):
        cluster = lax.broadcasted_iota(jnp.int32, (HOT, TW), 0) + k0
        onehot = jnp.concatenate(
            [(cluster == lab_ref[r:r + 1, :]).astype(F32).astype(BF16) for r in range(TH)], axis=1
        )
        hot_ref[k0:k0 + HOT, :] = onehot
        count_ref[:, k0:k0 + HOT] = dot(ones, onehot, ((1,), (1,)))


def filter_kernel(
    odd_ref, col_near_ref, col_far_ref, wide_ref, hot_ref, count_ref, *refs,
):
    a_ref, b_ref, c_ref, filt_ref, wb_ref, msg_ref = refs[5:]
    odd_col = odd_ref[1] == 1
    near = col_near_ref[0:COL_PIXELS, :].astype(F32).reshape(16, 8, C)
    far = col_far_ref[0:COL_PIXELS, :].astype(F32).reshape(16, 8, C)
    a_ref[:, 8:16, :] = jnp.where(odd_col, near, far)
    a_ref[:, 144:152, :] = jnp.where(odd_col, far, near)
    near = joined(col_near_ref, COL_PIXELS, 8)
    far = joined(col_far_ref, COL_PIXELS, 8)
    sides = unfolded(jnp.where(odd_col, far, near), jnp.where(odd_col, near, far))
    stack = normed_weights(wide_ref, sides)
    centre = stack[:, 0:TW].T
    sides = stack[:, TW:2 * TW].T
    spread_weights(wb_ref, jnp.concatenate([sides[120:128], centre[0:8]], axis=0), 8)
    spread_weights(wb_ref, jnp.concatenate([centre[120:128], sides[0:8]], axis=0), 136)
    sweep(1, (0, 1, 2, 15, 16, 17), wb_ref, a_ref, a_ref, b_ref)
    sweep(2, (0, 1, 2, 3, 14, 15, 16, 17), wb_ref, a_ref, b_ref, c_ref)
    sweep(3, (0, 1, 2, 3, 4, 13, 14, 15, 16, 17), wb_ref, a_ref, c_ref, b_ref)
    sweep(4, (1, 2, 3, 4, 5, 12, 13, 14, 15, 16), wb_ref, a_ref, b_ref, filt_ref)

    high, mid, low = split3(filt_ref[...])
    tall = ((0,), (0,))
    by_high = dot(high, jnp.concatenate([high, mid, low], axis=1), tall)
    by_mid = dot(mid, jnp.concatenate([high, mid], axis=1), tall)
    by_low = dot(low, high, tall)
    gram = by_high[:, 2 * C:] + by_low + by_mid[:, C:]
    gram = gram + (by_high[:, C:2 * C] + by_mid[:, :C])
    gram = gram + by_high[:, :C]

    pieces = jnp.concatenate([high, mid], axis=1)
    part = dot(hot_ref[...], pieces, ((1,), (0,)))
    part = part[:, C:] + part[:, :C]
    msg_ref[:, 0:ROWS_OF, :] = part.reshape(PARTS, ROWS_OF, C)
    msg_ref[:, ROWS_OF:ROWS_OF + 4, :] = gram.reshape(PARTS, 4, C)
    for p in range(PARTS):
        lanes = p * ROWS_OF // TW * TW
        msg_ref[p, ROWS_OF + 4:BLOCK, :] = count_ref[0:4, lanes:lanes + TW]


SCALARS = pl.BlockSpec(memory_space=pltpu.SMEM)
VECTORS = pl.BlockSpec(memory_space=pltpu.VMEM)


def pack_rows(odd, x, w):
    shape = jax.ShapeDtypeStruct((ROW_MSG, C), BF16)
    return pl.pallas_call(
        pack_rows_kernel,
        out_shape=(shape, shape),
        in_specs=[SCALARS] + [VECTORS] * 2,
        out_specs=(VECTORS,) * 2,
        compiler_params=pltpu.CompilerParams(vmem_limit_bytes=8 * 2**20),
    )(odd, x.reshape(TH * TW, C), w)


def pack_cols(odd, x, w, near, far):
    shape = jax.ShapeDtypeStruct((COL_MSG, C), BF16)
    return pl.pallas_call(
        pack_cols_kernel,
        out_shape=(
            shape,
            shape,
            jax.ShapeDtypeStruct((4, 24, TW), F32),
            jax.ShapeDtypeStruct((TH * TW, C), BF16),
        ),
        in_specs=[SCALARS] + [VECTORS] * 4,
        out_specs=(VECTORS,) * 4,
        scratch_shapes=[pltpu.VMEM((16, 8, C), F32)] * 2,
        compiler_params=pltpu.CompilerParams(vmem_limit_bytes=8 * 2**20),
    )(odd, x.reshape(TH * TW, C), w, near, far)


FIELD = jax.ShapeDtypeStruct((16, 160, C), F32)
BUFFERS = (
    FIELD,
    FIELD,
    FIELD,
    jax.ShapeDtypeStruct((TH * TW, C), F32),
    jax.ShapeDtypeStruct((4, 16, 160, C), F32),
)


def run_prepare(odd, x, near, far, wide, labels):
    outs = (
        jax.ShapeDtypeStruct((K, TH * TW), BF16),
        jax.ShapeDtypeStruct((8, K), F32),
    ) + BUFFERS
    return pl.pallas_call(
        prepare_kernel,
        out_shape=outs,
        in_specs=[SCALARS] + [VECTORS] * 5,
        out_specs=(VECTORS,) * 7,
        compiler_params=pltpu.CompilerParams(vmem_limit_bytes=16 * 2**20),
        cost_estimate=pl.CostEstimate(flops=2**27, bytes_accessed=2**23, transcendentals=0),
    )(odd, x, near, far, wide, labels)


def run_filter(odd, near, far, wide, hot, counts, *buffers):
    *_, filt, _, msg = pl.pallas_call(
        filter_kernel,
        in_specs=[SCALARS] + [VECTORS] * 10,
        out_shape=BUFFERS + (jax.ShapeDtypeStruct((PARTS, BLOCK, C), F32),),
        out_specs=(VECTORS,) * 6,
        input_output_aliases={6 + q: q for q in range(5)},
        compiler_params=pltpu.CompilerParams(vmem_limit_bytes=16 * 2**20),
    )(odd, near, far, wide, hot, counts, *buffers)
    return filt, msg


def eliminate(g_ref, panel=64, group=8):
    for p0 in range(0, C, panel):
        end = p0 + panel
        for i0 in range(p0, end, group):
            rows = end - i0
            left = g_ref[i0:end, 0:C]
            right = g_ref[i0:end, C:2 * C]
            sub = lax.broadcasted_iota(jnp.int32, (rows, C), 0)
            cols = [jnp.broadcast_to(left[:, i0 + k:i0 + k + 1], (rows, C)) for k in range(group)]
            lrow = [left[k:k + 1, :] for k in range(group)]
            rrow = [right[k:k + 1, :] for k in range(group)]
            a = [[cols[m][k:k + 1, :] for m in range(group)] for k in range(group)]
            for k in range(group):
                root = lax.rsqrt(a[k][k])
                s = [a[k][m] * root for m in range(group)]
                lrow[k] = lrow[k] * root
                rrow[k] = rrow[k] * root
                cols[k] = cols[k] * root
                for m in range(k + 1, group):
                    for n in range(m, group):
                        a[m][n] = a[m][n] - s[m] * s[n]
                    lrow[m] = lrow[m] - s[m] * lrow[k]
                    rrow[m] = rrow[m] - s[m] * rrow[k]
                    cols[m] = cols[m] - s[m] * cols[k]
            if rows > group:
                for k in range(group):
                    factor = jnp.where(sub >= group, cols[k], 0.0)
                    left = left - factor * lrow[k]
                    right = right - factor * rrow[k]
            for k in range(group):
                left = jnp.where(sub == k, lrow[k], left)
                right = jnp.where(sub == k, rrow[k], right)
            g_ref[i0:end, 0:C] = left
            g_ref[i0:end, C:2 * C] = right
        if end < C:
            uh, um, ul = split3(g_ref[p0:end, 0:C])
            fh, fm, fl = split3(g_ref[p0:end, :])
            lhs = jnp.concatenate([uh, um, ul, um, uh, uh], axis=0)
            rhs = jnp.concatenate([fl, fm, fh, fh, fm, fh], axis=0)
            update = dot(lhs, rhs, ((0,), (0,)))
            g_ref[end:C, :] = g_ref[end:C, :] - update[end:C, :]


def finish_kernel(msg_ref, filt_ref, best_ref, cent_ref, g_ref, c_ref, sem, *, total):
    for p in range(PARTS):
        g_ref[4 * p:4 * p + 4, 0:C] = msg_ref[p, ROWS_OF:ROWS_OF + 4, :]
    row = lax.broadcasted_iota(jnp.int32, (C, C), 0)
    col = lax.broadcasted_iota(jnp.int32, (C, C), 1)
    g_ref[:, C:2 * C] = jnp.where(row == col, 1.0, 0.0).astype(F32)

    eliminate(g_ref)
    inverse = g_ref[:, C:2 * C] * math.sqrt(total)
    ih, im, il = split3(inverse)
    lhs = jnp.concatenate([il, im, ih, im, ih, ih], axis=1)

    def times_inverse(x, transposed):
        xh, xm, xl = split3(x)
        rhs = jnp.concatenate([xh, xm, xl, xh, xm, xh], axis=1)
        if transposed:
            return dot(lhs, rhs, ((1,), (1,)))
        return dot(rhs, lhs, ((1,), (1,)))

    sums = msg_ref[:, 0:ROWS_OF, :].reshape(K, C)
    counts = jnp.concatenate(
        [jnp.broadcast_to(msg_ref[p, ROWS_OF + 4:ROWS_OF + 5, :], (C, C)).T for p in range(0, PARTS, 4)],
        axis=0,
    )
    c_ref[...] = times_inverse(sums, False) / (counts + 1.0)
    copy = pltpu.make_async_copy(c_ref, cent_ref, sem)
    copy.start()
    whitened_t = times_inverse(filt_ref[...], True)
    norms = jnp.sum(whitened_t * whitened_t, axis=0, keepdims=True)
    wh, wm, _ = split3(whitened_t)
    w_all = jnp.concatenate([wm, wh, wh], axis=0)
    cent = c_ref[...]
    cent_norm = jnp.sum(cent * cent, axis=1, keepdims=True)
    ch, cm, _ = split3(-2.0 * cent)
    c_all = jnp.concatenate([ch, cm, ch], axis=1)
    value = dot(c_all, w_all, ((1,), (0,))) + cent_norm
    best = jnp.min(value, axis=0, keepdims=True)
    result = (norms + best) / C
    for r in range(TH):
        best_ref[r:r + 1, :] = result[:, r * TW:(r + 1) * TW]
    copy.wait()


def run_finish(msg, filt, total):

    return pl.pallas_call(
        functools.partial(finish_kernel, total=total),
        out_shape=(
            jax.ShapeDtypeStruct((TH, TW), F32),
            jax.ShapeDtypeStruct((K, C), F32),
        ),
        out_specs=(VECTORS, pl.BlockSpec(memory_space=pltpu.HBM)),
        scratch_shapes=[pltpu.VMEM((C, 2 * C), F32), pltpu.VMEM((K, C), F32), pltpu.SemaphoreType.DMA],
        compiler_params=pltpu.CompilerParams(vmem_limit_bytes=32 * 2**20),
    )(msg, filt)


GY = ("xh", "y", "c")
GX = ("zh", "zl", "xl")


def swap(near, far, axes, size):
    near_pairs = [(i, i ^ 1) for i in range(size)]
    far_pairs = [(i, i + 1) for i in range(1, size - 1, 2)]
    far_pairs = far_pairs + [(b, a) for a, b in far_pairs]
    near = lax.ppermute(near, axes, near_pairs)
    return near, lax.ppermute(far, axes, far_pairs)


def exchange(x, axes):
    return lax.all_to_all(x, axes, 0, 0)


def spread(x, axes, count):
    return exchange(jnp.broadcast_to(x[None], (count,) + x.shape), axes)


def reduce_all(msg):
    piece = jnp.sum(exchange(msg, ("c", "xh", "y", "xl")), axis=0)
    piece = jnp.sum(spread(piece, "zl", 4), axis=0)
    piece = jnp.sum(spread(piece, "zh", 4), axis=0)
    half = spread(piece, ("xh", "y", "xl"), PARTS // 2)
    return lax.all_gather(half, "c", axis=0, tiled=True)


def on_device(embeddings, affinity, assignment):
    n_gy, n_gx = 16, 32
    odd = jnp.stack([lax.axis_index("c"), lax.axis_index("xl")]).astype(jnp.int32)
    rows = swap(*pack_rows(odd, embeddings, affinity), GY, n_gy)
    near, far, wide, pixels = pack_cols(odd, embeddings, affinity, *rows)
    prepared = run_prepare(odd, pixels, *rows, wide, assignment)
    cols = swap(near, far, GX, n_gx)
    filt, msg = run_filter(odd, *cols, wide, *prepared)
    msg = reduce_all(msg)
    return run_finish(msg, filt, TH * TW * n_gy * n_gx)


def solution(mesh):
    inner = Mesh(mesh.devices.reshape(2, 4, 2, 4, 4, 2), GY + GX)
    return jax.shard_map(
        on_device,
        mesh=inner,
        in_specs=(P(GY, GX, None), P(None, GY, GX), P(GY, GX)),
        out_specs=(P(GY, GX), P()),
        check_vma=False,
    )
```
